256 devices in a mesh: acq: 32 (over z, x_lo, core), strip: 8 (over x_hi, y).
Axes of the slice: x: 4 (x_hi: 2, x_lo: 2; x = x_hi * 2 + x_lo), y: 4, z: 8, core: 2. Of those that a mesh axis runs over, the one named last changes fastest.
Arguments:
- echoes: float32 [128, 2, 256, 2048], P('acq', None, 'strip'), may hold values from -12 to 12
- pair_list: int32 [128, 2], P('acq'), may hold values from 0 to 127, as said below
- phase_ramps: int32 [128, 2], P('acq'), may hold values from -4 to 4
Outputs:
- coherence: float32 [128, 2, 256, 128], P('acq', None, 'strip')
The draws below stay inside these ranges and needn't reach their ends.
Inputs may be any that keep to these rules, and one draw needn't show every extreme that they name: `pair_list`: row p's secondary lies in block p // 4 of 4 acquisitions (acquisitions k * 4 to k * 4 + 3 form block k), and every acquisition of that block is the secondary of 1 of its rows, in order of row. The reference differs from the secondary; in block 0 it lies in block 0, elsewhere it is 1 to 3 acquisitions before the secondary. The first acquisition of every block but block 0 has its reference in the block before.
All inputs are finite; a program needn't handle non-finite values.
Results may differ from the reference program's by a relative error of at most 0.0003.
Values sent between devices are 32-bit elements; how exact they have to be, the bound alone decides.
A program may use at most 64 MiB of HBM per device.

```python
import math
import jax
import jax.numpy as jnp
from jax import lax

ACQ_DEV = 4
PAIRS_DEV = 4
RG = 2048
ACQS = 128
PAIRS = 128
AZ = 256


def draw_echoes(key, part):
    subkeys = jax.random.split(key, 3)
    scenery = jax.random.normal(subkeys[0], (1, 2, AZ, RG), jnp.float32)
    gain_values = jax.random.uniform(subkeys[1], (ACQS, 1, 1, 1), jnp.float32, 0.6, 1.4)
    noise_part = 0.7 * jax.random.normal(subkeys[2], (ACQS, 2, AZ, RG), jnp.float32)
    values = scenery * gain_values + noise_part
    return jnp.clip(values, -12.0, 12.0)


def draw_pair_list(key, part):
    row_ids = jnp.arange(PAIRS, dtype=jnp.int32)
    row_group = row_ids // PAIRS_DEV
    slot_index = row_ids % ACQ_DEV
    lag_steps = jax.random.randint(key, (PAIRS,), 1, ACQ_DEV, dtype=jnp.int32)
    second = row_group * ACQ_DEV + slot_index
    first_index = jnp.where(row_group == 0, jnp.mod(slot_index - lag_steps, ACQ_DEV), second - lag_steps)
    return jnp.stack([first_index, second], axis=1).astype(jnp.int32)


def place_ends(result, rng, smallest, high):
    shape = result.shape
    spot = [jax.random.randint(jax.random.fold_in(rng, axis), (), 0, shape[axis]) for axis in range(len(shape))]
    result = result.at[tuple(spot)].set(smallest)
    longest = shape.index(max(shape))
    spot[longest] = (spot[longest] + 1) % shape[longest]
    return result.at[tuple(spot)].set(high)


def setup_inputs(seed: int = 0) -> dict:
    streams_of = jax.random.split(jax.random.key(seed), 4)
    return {
        "echoes": draw_echoes(jax.random.fold_in(streams_of[3], 71), 0),
        "pair_list": draw_pair_list(jax.random.fold_in(streams_of[3], 71), 0),
        "phase_ramps": place_ends(jax.random.randint(streams_of[2], (PAIRS, 2), -4, 5), jax.random.fold_in(streams_of[2], 1), -4, 4).astype(jnp.int32),
    }


def range_taps():
    offsets = jnp.arange(64, dtype=jnp.int32) - 32
    shifted = offsets.astype(jnp.float32) + 0.5
    return jnp.exp(-(shifted * shifted) / 512.0).reshape(4, 16)

def azimuth_taps():
    offsets = jnp.arange(17, dtype=jnp.int32) - 8
    values = offsets.astype(jnp.float32)
    return jnp.exp(-(values * values) / 32.0)

def interfere(first_piece, second_piece, ramp_pair, line_index, range_index, range_count, line_count):
    real_first, imag_first = (first_piece[0], first_piece[1])
    real_second, imag_second = (second_piece[0], second_piece[1])
    real_part = real_first * real_second + imag_first * imag_second
    imag_part = imag_first * real_second - real_first * imag_second
    range_turns = jnp.mod(ramp_pair[0] * range_index, range_count).astype(jnp.float32) / float(range_count)
    line_turns = jnp.mod(ramp_pair[1] * line_index, line_count).astype(jnp.float32) / float(line_count)
    angles = 2.0 * math.pi * (range_turns[None, :] + line_turns[:, None])
    cosine = jnp.cos(angles)
    sine = jnp.sin(angles)
    return jnp.stack([real_part * cosine + imag_part * sine, imag_part * cosine - real_part * sine, real_first * real_first + imag_first * imag_first, real_second * real_second + imag_second * imag_second])

def range_look(fields):
    outputs = fields.shape[2] // 16
    blocked = fields.reshape(fields.shape[0], fields.shape[1], outputs, 16)
    blocked = jnp.pad(blocked, ((0, 0), (0, 0), (2, 2), (0, 0)))
    tap_weights = range_taps()
    summed = jnp.zeros((fields.shape[0], fields.shape[1], outputs), jnp.float32)
    for offset in range(4):
        summed = summed + jnp.einsum('flok,k->flo', blocked[:, :, offset:offset + outputs, :], tap_weights[offset], precision=lax.Precision.HIGHEST)
    return summed

def azimuth_look(fields):
    line_total = fields.shape[1]
    padded = jnp.pad(fields, ((0, 0), (8, 8), (0, 0)))
    tap_weights = azimuth_taps()
    summed = jnp.zeros(fields.shape, jnp.float32)
    for offset in range(17):
        summed = summed + tap_weights[offset] * padded[:, offset:offset + line_total, :]
    return summed

def normalized(summed):
    scaling = 1.0 / jnp.sqrt(summed[2] * summed[3] + 1e-06)
    return jnp.stack([summed[0] * scaling, summed[1] * scaling])

def reference(echoes, pair_list, phase_ramps):
    range_index = jnp.arange(RG, dtype=jnp.int32)
    line_index = jnp.arange(AZ, dtype=jnp.int32)

    def per_pair(items):
        pair_row, ramp_pair = items
        first_piece = echoes[pair_row[0]]
        second_piece = echoes[pair_row[1]]
        fields = interfere(first_piece, second_piece, ramp_pair, line_index, range_index, RG, AZ)
        return normalized(azimuth_look(range_look(fields)))
    return lax.map(per_pair, (pair_list, phase_ramps))
```

```python
import functools
import math

import jax
import jax.numpy as jnp
from jax import lax
from jax.experimental import pallas as pl
from jax.experimental.pallas import tpu as pltpu
from jax.sharding import PartitionSpec as P

MESH = pl.DeviceIdType.MESH
F32, BF16, I32 = jnp.float32, jnp.bfloat16, jnp.int32
LINES = 8
PARTS = 2
STEP = 16
TILE = 256


def iota(shape, dim):
    return lax.broadcasted_iota(I32, shape, dim)


def split(value):
    high = value.astype(BF16)
    return high, (value - high.astype(F32)).astype(BF16)


def turns(count, whole):
    angle = (count & (whole - 1)).astype(F32) * (2.0 * math.pi / whole)
    return jnp.cos(angle), jnp.sin(angle)


def group_order(groups):
    return [0, groups - 1] + list(range(1, groups - 1))


def kernel(
    sizes, echoes, pairs, ramps, out, pieces, pair_mem, ramp_mem, weights, table, line_table,
    fields, sums, looks, above, below, send_sem, recv_sem, own_sem, small_sem, edge_send, edge_recv,
):
    acqs, groups, width, acq_size, strip_size = sizes
    reach = acqs - 1
    part_width = width // PARTS
    outputs = width // STEP
    lines = groups * LINES
    acq, strip = lax.axis_index("acq"), lax.axis_index("strip")
    has_next, has_previous = acq < acq_size - 1, acq > 0
    has_below, has_above = strip < strip_size - 1, strip > 0
    chunks = [(g, h) for g in group_order(groups) for h in range(PARTS)]

    barrier = pltpu.get_barrier_semaphore()

    def greet(condition, target):
        @pl.when(condition)
        def _():
            pl.semaphore_signal(barrier, inc=1, device_id=target, device_id_type=MESH)

    greet(has_previous, {"acq": acq - 1})
    greet(has_next, {"acq": acq + 1})
    greet(has_above, {"strip": strip - 1})
    greet(has_below, {"strip": strip + 1})

    pair_copy = pltpu.make_async_copy(pairs, pair_mem, small_sem.at[0])
    ramp_copy = pltpu.make_async_copy(ramps, ramp_mem, small_sem.at[1])
    pair_copy.start()
    ramp_copy.start()

    def region(first, g, h):
        return echoes.at[
            pl.ds(first, acqs - first), :, pl.ds(g * LINES, LINES), pl.ds(h * part_width, part_width)
        ]

    own, sent = [], []
    for i, (g, h) in enumerate(chunks):
        own.append(
            pltpu.make_async_copy(
                region(0, g, h), pieces[i].at[pl.ds(reach, acqs)], own_sem.at[i]
            )
        )
        sent.append(
            pltpu.make_async_remote_copy(
                region(1, g, h), pieces[i].at[pl.ds(0, reach)], send_sem.at[i], recv_sem.at[i],
                device_id={"acq": acq + 1}, device_id_type=MESH,
            )
        )

    neighbours = sum(c.astype(I32) for c in (has_next, has_previous, has_below, has_above))
    pl.semaphore_wait(barrier, neighbours)

    @pl.when(has_next)
    def _():
        for copy in sent:
            copy.start()

    for copy in own:
        copy.start()

    @pl.loop(0, width // TILE)
    def _(t):
        rows = pl.ds(pl.multiple_of(t * TILE, TILE), TILE)
        offset = iota((TILE, outputs), 0) + t * TILE - STEP * iota((TILE, outputs), 1)
        shifted = offset.astype(F32) + 0.5
        taps = jnp.exp(-(shifted * shifted) / 512.0)
        high, low = split(jnp.where((offset >= -32) & (offset < 32), taps, 0.0))
        weights[rows, 0:outputs] = high
        weights[rows, outputs : 2 * outputs] = low

    pair_copy.wait()
    ramp_copy.wait()

    @pl.loop(0, acqs)
    def _(p):
        cosine, sine = turns(ramp_mem[p, 0] * iota((LINES, width), 1), width)
        table[p, 0] = cosine
        table[p, 1] = sine
        line = strip * lines + iota((lines, outputs), 0)
        cosine, sine = turns(ramp_mem[p, 1] * line, lines * strip_size)
        line_table[p, 0] = cosine
        line_table[p, 1] = sine

    @pl.when(jnp.logical_not(has_above))
    def _():
        above[...] = jnp.zeros_like(above)

    @pl.when(jnp.logical_not(has_below))
    def _():
        below[...] = jnp.zeros_like(below)

    slots = [jnp.clip(pair_mem[p, 0] - acq * acqs + reach, 0, reach + acqs - 1) for p in range(acqs)]
    half = acqs * 4 * LINES
    edge_up = pltpu.make_async_remote_copy(
        looks[0], below, edge_send.at[0], edge_recv.at[0],
        device_id={"strip": strip - 1}, device_id_type=MESH,
    )
    edge_down = pltpu.make_async_remote_copy(
        looks[groups - 1], above, edge_send.at[1], edge_recv.at[1],
        device_id={"strip": strip + 1}, device_id_type=MESH,
    )

    for i, (g, h) in enumerate(chunks):
        own[i].wait()

        @pl.when(has_previous)
        def _():
            sent[i].wait_recv()

        piece = pieces[i]
        for t in range(part_width // TILE):
            here = pl.ds(t * TILE, TILE)
            there = pl.ds(h * part_width + t * TILE, TILE)
            for p in range(acqs):
                a, b = piece[slots[p], 0, :, here], piece[slots[p], 1, :, here]
                c, d = piece[reach + p, 0, :, here], piece[reach + p, 1, :, here]
                cosine, sine = table[p, 0, :, there], table[p, 1, :, there]
                x, y = a * c + b * d, b * c - a * d
                value = jnp.concatenate(
                    [x * cosine + y * sine, y * cosine - x * sine, a * a + b * b, c * c + d * d]
                )
                high, low = split(value)
                fields[pl.ds(p * 4 * LINES, 4 * LINES), here] = high
                fields[pl.ds(half + p * 4 * LINES, 4 * LINES), here] = low
        product = jnp.dot(
            fields[...], weights[pl.ds(h * part_width, part_width), :], preferred_element_type=F32
        )
        part = (
            product[:half, :outputs] + product[:half, outputs:] + product[half:, :outputs]
        )
        if h == 0:
            sums[...] = part
        elif h < PARTS - 1:
            sums[...] += part
        if h == PARTS - 1:
            whole = sums[...] + part if PARTS > 1 else part
            whole = whole.reshape(acqs, 4, LINES, outputs)
            for p in range(acqs):
                now = pl.ds(g * LINES, LINES)
                cosine, sine = line_table[p, 0, now, :], line_table[p, 1, now, :]
                x, y = whole[p, 0], whole[p, 1]
                looks[g][p, 0] = x * cosine + y * sine
                looks[g][p, 1] = y * cosine - x * sine
                looks[g][p, 2] = whole[p, 2]
                looks[g][p, 3] = whole[p, 3]
            if g == 0:

                @pl.when(has_above)
                def _():
                    edge_up.start()

            if g == groups - 1:

                @pl.when(has_below)
                def _():
                    edge_down.start()

    @pl.when(has_above)
    def _():
        edge_down.wait_recv()

    @pl.when(has_below)
    def _():
        edge_up.wait_recv()

    offset = iota((lines, lines + 2 * LINES), 1) - iota((lines, lines + 2 * LINES), 0) - LINES
    value = offset.astype(F32)
    band = jnp.where(
        (offset >= -LINES) & (offset <= LINES), jnp.exp(-(value * value) / 32.0), 0.0
    )
    high, low = split(band)
    band = jnp.concatenate([high, high, low], axis=1)
    for p in range(acqs):
        summed = []
        for k in range(0, 4, 2):
            value = jnp.concatenate(
                [
                    jnp.concatenate([source[p, k], source[p, k + 1]], axis=1)
                    for source in (above, *looks, below)
                ]
            )
            high, low = split(value)
            value = jnp.concatenate([high, low, high])
            value = jnp.dot(band, value, preferred_element_type=F32)
            summed += [value[:, :outputs], value[:, outputs:]]
        scaling = 1.0 / jnp.sqrt(summed[2] * summed[3] + 1e-06)
        out[p, 0] = summed[0] * scaling
        out[p, 1] = summed[1] * scaling

    @pl.when(has_next)
    def _():
        for copy in sent:
            copy.wait_send()

    @pl.when(has_above)
    def _():
        edge_up.wait_send()

    @pl.when(has_below)
    def _():
        edge_down.wait_send()


def body(echoes, pair_list, phase_ramps):
    acqs, _, lines, width = echoes.shape
    groups = lines // LINES
    outputs = width // STEP
    chunks = groups * PARTS
    sizes = (acqs, groups, width, lax.axis_size("acq"), lax.axis_size("strip"))
    dma = pltpu.SemaphoreType.DMA
    look = pltpu.VMEM((acqs, 4, LINES, outputs), F32)
    return pl.pallas_call(
        functools.partial(kernel, sizes),
        out_shape=jax.ShapeDtypeStruct((acqs, 2, lines, outputs), F32),
        in_specs=[pl.BlockSpec(memory_space=pl.ANY)] * 3,
        out_specs=pl.BlockSpec(memory_space=pltpu.VMEM),
        scratch_shapes=[
            [pltpu.VMEM((2 * acqs - 1, 2, LINES, width // PARTS), F32) for _ in range(chunks)],
            pltpu.SMEM(pair_list.shape, I32),
            pltpu.SMEM(phase_ramps.shape, I32),
            pltpu.VMEM((width, 2 * outputs), BF16),
            pltpu.VMEM((acqs, 2, LINES, width), F32),
            pltpu.VMEM((acqs, 2, lines, outputs), F32),
            pltpu.VMEM((2 * acqs * 4 * LINES, width // PARTS), BF16),
            pltpu.VMEM((acqs * 4 * LINES, outputs), F32),
            [look for _ in range(groups)],
            look,
            look,
            dma((chunks,)),
            dma((chunks,)),
            dma((chunks,)),
            dma((2,)),
            dma((2,)),
            dma((2,)),
        ],
        compiler_params=pltpu.CompilerParams(collective_id=0, has_side_effects=True),
    )(echoes, pair_list, phase_ramps)


def solution(mesh):
    return jax.shard_map(
        body,
        mesh=mesh,
        in_specs=(P("acq", None, "strip", None), P("acq", None), P("acq", None)),
        out_specs=P("acq", None, "strip", None),
        check_vma=False,
    )
```

```python
import functools
import math

import jax
import jax.numpy as jnp
from jax import lax
from jax.experimental import pallas as pl
from jax.experimental.pallas import tpu as pltpu
from jax.sharding import PartitionSpec as P

MESH = pl.DeviceIdType.MESH
F32, BF16, I32 = jnp.float32, jnp.bfloat16, jnp.int32
LINES = 8
PARTS = (1024, 1024)
LAST_PARTS = (1024, 768, 256)
DEPTH = 3
RELAY_AT = 4
CHIPS = 4
STEP = 16
TILE = 256


def iota(shape, dim):
    return lax.broadcasted_iota(I32, shape, dim)


def split(value):
    high = value.astype(BF16)
    return high, (value - high.astype(F32)).astype(BF16)


def turns(count, whole):
    angle = (count & (whole - 1)).astype(F32) * (2.0 * math.pi / whole)
    return jnp.cos(angle), jnp.sin(angle)


def group_order(groups):
    return [0, groups - 1] + list(range(1, groups - 1))


def chunk_list(groups):
    chunks = []
    for g in group_order(groups):
        parts = LAST_PARTS if g == group_order(groups)[-1] else PARTS
        start = 0
        for i, count in enumerate(parts):
            chunks.append((g, start, count, i == 0, i == len(parts) - 1))
            start += count
    return chunks


def kernel(
    sizes, echoes, pairs, ramps, out, pieces, pair_mem, ramp_mem, weights, table, line_table,
    fields, sums, partial, looks, above, below, relayed, send_sem, recv_sem, own_sem, small_sem, edge_send, edge_recv,
    relay_send, relay_recv,
):
    acqs, groups, width, acq_size, strip_size = sizes
    reach = acqs - 1
    outputs = width // STEP
    lines = groups * LINES
    acq, strip = lax.axis_index("acq"), lax.axis_index("strip")
    has_next, has_previous = acq < acq_size - 1, acq > 0
    has_below, has_above = strip < strip_size - 1, strip > 0
    place = lax.rem(acq, CHIPS)
    middle = strip_size // 2
    on_second = place >= CHIPS // 2
    relay_down, relay_up = on_second & (strip == middle - 1), on_second & (strip == middle)
    direct_down = has_below & jnp.logical_not(relay_down)
    direct_up = has_above & jnp.logical_not(relay_up)
    relays_up, relays_down = (place == 0) & (strip == 0), (place == 0) & (strip == strip_size - 1)
    first_strip, last_strip = jnp.int32(0), jnp.int32(strip_size - 1)
    chunks = chunk_list(groups)
    last_group = group_order(groups)[-1]

    barrier = pltpu.get_barrier_semaphore()

    def greet(condition, target):
        @pl.when(condition)
        def _():
            pl.semaphore_signal(barrier, inc=1, device_id=target, device_id_type=MESH)

    greet(has_previous, {"acq": acq - 1})
    greet(has_above & jnp.logical_not(relay_up), {"strip": strip - 1})
    greet(has_below & jnp.logical_not(relay_down), {"strip": strip + 1})
    greet(relay_up, {"acq": acq - place, "strip": last_strip})
    greet(relay_down, {"acq": acq - place, "strip": first_strip})
    for j in range(2):
        greet(relays_up, {"acq": acq + CHIPS // 2 + j, "strip": jnp.int32(middle)})
        greet(relays_down, {"acq": acq + CHIPS // 2 + j, "strip": jnp.int32(middle - 1)})

    pair_copy = pltpu.make_async_copy(pairs, pair_mem, small_sem.at[0])
    ramp_copy = pltpu.make_async_copy(ramps, ramp_mem, small_sem.at[1])
    pair_copy.start()
    ramp_copy.start()

    def region(first, g, start, count):
        return echoes.at[
            pl.ds(first, acqs - first), :, pl.ds(g * LINES, LINES), pl.ds(start, count)
        ]

    own, sent = [], []
    for i, (g, start, count, _, _) in enumerate(chunks):
        own.append(
            pltpu.make_async_copy(
                region(0, g, start, count), pieces[i].at[pl.ds(reach, acqs)], own_sem.at[i]
            )
        )
        sent.append(
            pltpu.make_async_remote_copy(
                region(1, g, start, count), pieces[i].at[pl.ds(0, reach)], send_sem.at[i], recv_sem.at[i],
                device_id={"acq": acq + 1}, device_id_type=MESH,
            )
        )

    targets = (has_next, direct_down, direct_up, relay_down, relay_up)
    targets += (relays_up, relays_down, relays_up, relays_down)
    neighbours = sum(c.astype(I32) for c in targets)
    pl.semaphore_wait(barrier, neighbours)

    @pl.when(has_next)
    def _():
        for copy in sent[:DEPTH]:
            copy.start()

    for copy in own:
        copy.start()

    @pl.loop(0, width // TILE)
    def _(t):
        rows = pl.ds(pl.multiple_of(t * TILE, TILE), TILE)
        offset = iota((TILE, outputs), 0) + t * TILE - STEP * iota((TILE, outputs), 1)
        shifted = offset.astype(F32) + 0.5
        taps = jnp.exp(-(shifted * shifted) / 512.0)
        high, low = split(jnp.where((offset >= -32) & (offset < 32), taps, 0.0))
        weights[rows, 0:outputs] = high
        weights[rows, outputs : 2 * outputs] = low

    pair_copy.wait()
    ramp_copy.wait()

    @pl.loop(0, acqs)
    def _(p):
        cosine, sine = turns(ramp_mem[0, p] * iota((LINES, width), 1), width)
        table[p, 0] = cosine
        table[p, 1] = sine
        line = strip * lines + iota((lines, outputs), 0)
        cosine, sine = turns(ramp_mem[1, p] * line, lines * strip_size)
        line_table[p, 0] = cosine
        line_table[p, 1] = sine

    @pl.when(jnp.logical_not(has_above))
    def _():
        above[...] = jnp.zeros_like(above)

    @pl.when(jnp.logical_not(has_below))
    def _():
        below[...] = jnp.zeros_like(below)

    slots = [jnp.clip(pair_mem[0, p] - acq * acqs + reach, 0, reach + acqs - 1) for p in range(acqs)]
    half = acqs * 4 * LINES
    edge_up = pltpu.make_async_remote_copy(
        looks[0], below, edge_send.at[0], edge_recv.at[0],
        device_id={"strip": strip - 1}, device_id_type=MESH,
    )
    edge_down = pltpu.make_async_remote_copy(
        looks[groups - 1], above, edge_send.at[1], edge_recv.at[1],
        device_id={"strip": strip + 1}, device_id_type=MESH,
    )

    offset = iota((lines, lines + 2 * LINES), 1) - iota((lines, lines + 2 * LINES), 0) - LINES
    value = offset.astype(F32)
    taps = jnp.where((offset >= -LINES) & (offset <= LINES), jnp.exp(-(value * value) / 32.0), 0.0)
    taps_high = taps.astype(BF16).astype(F32)
    taps_low = taps - taps_high

    def azimuth(p, k, blocks):
        value = jnp.concatenate(
            [
                jnp.concatenate([source[p, k], source[p, k + 1]], axis=1)
                for _, source in blocks
            ]
        )
        high = value.astype(BF16).astype(F32)
        columns = [
            jnp.concatenate([part[:, j * LINES : (j + 1) * LINES] for j, _ in blocks], axis=1)
            for part in (taps_high, taps_low)
        ]
        left = jnp.concatenate([columns[0], columns[0], columns[1]], axis=1)
        right = jnp.concatenate([high, value - high, high])
        return jnp.dot(left.astype(BF16), right.astype(BF16), preferred_element_type=F32)

    lane = jnp.maximum(place - CHIPS // 2, 0)

    def to_relay(source, target):
        return pltpu.make_async_remote_copy(
            source, relayed.at[lane], edge_send.at[2], relay_recv.at[lane],
            device_id={"acq": acq - place, "strip": target}, device_id_type=MESH,
        )

    to_relay_up = to_relay(looks[0], first_strip)
    to_relay_down = to_relay(looks[groups - 1], last_strip)

    def from_relay(j, target, room, recv):
        return pltpu.make_async_remote_copy(
            relayed.at[j], room, relay_send.at[j], edge_recv.at[recv],
            device_id={"acq": acq + CHIPS // 2 + j, "strip": jnp.int32(target)}, device_id_type=MESH,
        )

    from_relay_up = [from_relay(j, middle - 1, below, 0) for j in range(2)]
    from_relay_down = [from_relay(j, middle, above, 1) for j in range(2)]
    from_second = [
        pltpu.make_async_remote_copy(
            relayed.at[j], relayed.at[j], relay_send.at[j], relay_recv.at[j],
            device_id={"acq": acq}, device_id_type=MESH,
        )
        for j in range(2)
    ]

    for i, (g, start, count, first_part, last_part) in enumerate(chunks):
        if i == RELAY_AT:
            for condition, copies in ((relays_up, from_relay_up), (relays_down, from_relay_down)):

                @pl.when(condition)
                def _():
                    for j, copy in enumerate(copies):
                        from_second[j].wait_recv()
                        copy.start()

        if i + DEPTH < len(chunks):

            @pl.when(has_next)
            def _():
                sent[i].wait_send()
                sent[i + DEPTH].start()

        if i == len(chunks) - 1:

            @pl.when(has_above)
            def _():
                edge_down.wait_recv()

            @pl.when(has_below)
            def _():
                edge_up.wait_recv()

            blocks = [(0, above), (groups + 1, below)]
            blocks += [(j + 1, looks[j]) for j in range(groups) if j != last_group]
            for p in range(acqs):
                for k in range(0, 4, 2):
                    partial[p, k // 2] = azimuth(p, k, blocks)

        own[i].wait()

        @pl.when(has_previous)
        def _():
            sent[i].wait_recv()

        piece = pieces[i]
        for t in range(count // TILE):
            here = pl.ds(t * TILE, TILE)
            there = pl.ds(start + t * TILE, TILE)
            for p in range(acqs):
                a, b = piece[slots[p], 0, :, here], piece[slots[p], 1, :, here]
                c, d = piece[reach + p, 0, :, here], piece[reach + p, 1, :, here]
                cosine, sine = table[p, 0, :, there], table[p, 1, :, there]
                x, y = a * c + b * d, b * c - a * d
                value = jnp.concatenate(
                    [x * cosine + y * sine, y * cosine - x * sine, a * a + b * b, c * c + d * d]
                )
                high, low = split(value)
                fields[pl.ds(p * 4 * LINES, 4 * LINES), here] = high
                fields[pl.ds(half + p * 4 * LINES, 4 * LINES), here] = low
        product = jnp.dot(
            fields[:, 0:count], weights[pl.ds(start, count), :], preferred_element_type=F32
        )
        part = (
            product[:half, :outputs] + product[:half, outputs:] + product[half:, :outputs]
        )
        if first_part:
            sums[...] = part
        elif not last_part:
            sums[...] += part
        if last_part:
            whole = part if first_part else sums[...] + part
            whole = whole.reshape(acqs, 4, LINES, outputs)
            for p in range(acqs):
                now = pl.ds(g * LINES, LINES)
                cosine, sine = line_table[p, 0, now, :], line_table[p, 1, now, :]
                x, y = whole[p, 0], whole[p, 1]
                looks[g][p, 0] = x * cosine + y * sine
                looks[g][p, 1] = y * cosine - x * sine
                looks[g][p, 2] = whole[p, 2]
                looks[g][p, 3] = whole[p, 3]
            if g == 0:

                @pl.when(direct_up)
                def _():
                    edge_up.start()

                @pl.when(relay_up)
                def _():
                    to_relay_up.start()

            if g == groups - 1:

                @pl.when(direct_down)
                def _():
                    edge_down.start()

                @pl.when(relay_down)
                def _():
                    to_relay_down.start()

    for p in range(acqs):
        summed = []
        for k in range(0, 4, 2):
            value = partial[p, k // 2] + azimuth(p, k, [(last_group + 1, looks[last_group])])
            summed += [value[:, :outputs], value[:, outputs:]]
        scaling = 1.0 / jnp.sqrt(summed[2] * summed[3] + 1e-06)
        out[p, 0] = summed[0] * scaling
        out[p, 1] = summed[1] * scaling

    @pl.when(has_next)
    def _():
        for copy in sent[-DEPTH:]:
            copy.wait_send()

    for condition, copies in (
        (direct_up, [edge_up]),
        (direct_down, [edge_down]),
        (relay_up, [to_relay_up]),
        (relay_down, [to_relay_down]),
        (relays_up, from_relay_up),
        (relays_down, from_relay_down),
    ):

        @pl.when(condition)
        def _():
            for copy in copies:
                copy.wait_send()


def body(echoes, pair_list, phase_ramps):
    acqs, _, lines, width = echoes.shape
    groups = lines // LINES
    outputs = width // STEP
    chunks = chunk_list(groups)
    sizes = (acqs, groups, width, lax.axis_size("acq"), lax.axis_size("strip"))
    dma = pltpu.SemaphoreType.DMA
    look = pltpu.VMEM((acqs, 4, LINES, outputs), F32)
    return pl.pallas_call(
        functools.partial(kernel, sizes),
        out_shape=jax.ShapeDtypeStruct((acqs, 2, lines, outputs), F32),
        in_specs=[pl.BlockSpec(memory_space=pl.ANY)] * 3,
        out_specs=pl.BlockSpec(memory_space=pltpu.VMEM),
        scratch_shapes=[
            [pltpu.VMEM((2 * acqs - 1, 2, LINES, c[2]), F32) for c in chunks],
            pltpu.SMEM((2, acqs), I32),
            pltpu.SMEM((2, acqs), I32),
            pltpu.VMEM((width, 2 * outputs), BF16),
            pltpu.VMEM((acqs, 2, LINES, width), F32),
            pltpu.VMEM((acqs, 2, lines, outputs), F32),
            pltpu.VMEM((2 * acqs * 4 * LINES, max(c[2] for c in chunks)), BF16),
            pltpu.VMEM((acqs * 4 * LINES, outputs), F32),
            pltpu.VMEM((acqs, 2, lines, 2 * outputs), F32),
            [look for _ in range(groups)],
            look,
            look,
            pltpu.VMEM((2, acqs, 4, LINES, outputs), F32),
            dma((len(chunks),)),
            dma((len(chunks),)),
            dma((len(chunks),)),
            dma((2,)),
            dma((3,)),
            dma((2,)),
            dma((2,)),
            dma((2,)),
        ],
        compiler_params=pltpu.CompilerParams(collective_id=0, has_side_effects=True, vmem_limit_bytes=16 << 20),
    )(*(pltpu.with_memory_space_constraint(v, pltpu.HBM) for v in (echoes, pair_list.T, phase_ramps.T)))


def solution(mesh):
    return jax.shard_map(
        body,
        mesh=mesh,
        in_specs=(P("acq", None, "strip", None), P("acq", None), P("acq", None)),
        out_specs=P("acq", None, "strip", None),
        check_vma=False,
    )
```

```python
import functools
import math

import jax
import jax.numpy as jnp
from jax import lax
from jax.experimental import pallas as pl
from jax.experimental.pallas import tpu as pltpu
from jax.sharding import PartitionSpec as P

MESH = pl.DeviceIdType.MESH
F32, BF16, I32 = jnp.float32, jnp.bfloat16, jnp.int32
LINES = 8
PARTS = (1024, 1024)
LAST_PARTS = (1024, 768, 256)
DEPTH = 3
RELAY_AT = 3
CHIPS = 4
STEP = 16
TILE = 256


def iota(shape, dim):
    return lax.broadcasted_iota(I32, shape, dim)


def split(value):
    high = value.astype(BF16)
    return high, (value - high.astype(F32)).astype(BF16)


def turns(count, whole):
    angle = (count & (whole - 1)).astype(F32) * (2.0 * math.pi / whole)
    return jnp.cos(angle), jnp.sin(angle)


def chunk_list(groups):
    chunks = []
    for g in range(groups):
        parts = LAST_PARTS if g == groups - 1 else PARTS
        start = 0
        for i, count in enumerate(parts):
            chunks.append((g, start, count, i == 0, i == len(parts) - 1))
            start += count
    return chunks


def kernel(
    sizes, echoes, pairs, ramps, out, pieces, pair_mem, ramp_mem, weights, table, line_table, fields,
    sums, partial, looks, edges, relayed, send_sem, recv_sem, own_sem, small_sem, edge_send, edge_recv,
    relay_recv,
):
    acqs, groups, width, acq_size, strip_size = sizes
    reach = acqs - 1
    outputs = width // STEP
    lines = groups * LINES
    acq, strip = lax.axis_index("acq"), lax.axis_index("strip")
    has_next, has_previous = acq < acq_size - 1, acq > 0
    place = lax.rem(acq, CHIPS)
    middle, last = strip_size // 2, strip_size - 1

    upper = strip < middle
    inner = jnp.where(upper, strip + 1, strip - 1)
    outer = jnp.where(upper, strip - 1, strip + 1)
    outer_room = jnp.where(upper, 0, 1)
    inner_room = 1 - outer_room
    has_outer = (strip > 0) & (strip < last)
    order = [jnp.where(upper, groups - 1, 0), jnp.where(upper, 0, groups - 1), *range(1, groups - 1)]
    first_line = [pl.multiple_of(g * LINES, LINES) for g in order]

    crosses = ((strip == middle - 1) | (strip == middle)) & (place != 0)
    down_relay = jnp.where(place == 1, middle - 2, jnp.where(place == 2, last, last - 1))
    relay_out = jnp.where(upper, down_relay, last - down_relay)
    relay_in = last - relay_out
    depth = jnp.where(upper, strip, last - strip)
    relays = (place == 0) & (depth < middle - 1)
    from_place = jnp.where(depth == middle - 2, 1, jnp.where(depth == 0, 2, 3))
    relays_down = upper == (from_place == 1)
    relay_from = jnp.where(relays_down, middle - 1, middle)
    relay_to = jnp.where(relays_down, middle, middle - 1)
    relay_room = jnp.where(relays_down, 0, 1)
    chunks = chunk_list(groups)

    barrier = pltpu.get_barrier_semaphore()

    def greet(condition, target):
        @pl.when(condition)
        def _():
            pl.semaphore_signal(barrier, inc=1, device_id=target, device_id_type=MESH)

    greet(has_previous, {"acq": acq - 1})
    greet(jnp.logical_not(crosses), {"strip": inner})
    greet(crosses, {"acq": acq - place, "strip": relay_in})
    greet(has_outer, {"strip": outer})
    greet(relays, {"acq": acq + from_place, "strip": relay_from})

    pair_copy = pltpu.make_async_copy(pairs, pair_mem, small_sem.at[0])
    ramp_copy = pltpu.make_async_copy(ramps, ramp_mem, small_sem.at[1])
    pair_copy.start()
    ramp_copy.start()

    def region(first, g, start, count):
        return echoes.at[
            pl.ds(first, acqs - first), :, pl.ds(first_line[g], LINES), pl.ds(start, count)
        ]

    own, sent = [], []
    for i, (g, start, count, _, _) in enumerate(chunks):
        own.append(
            pltpu.make_async_copy(
                region(0, g, start, count), pieces[i].at[pl.ds(reach, acqs)], own_sem.at[i]
            )
        )
        sent.append(
            pltpu.make_async_remote_copy(
                region(1, g, start, count), pieces[i].at[pl.ds(0, reach)], send_sem.at[i], recv_sem.at[i],
                device_id={"acq": acq + 1}, device_id_type=MESH,
            )
        )

    neighbours = 1 + sum(c.astype(I32) for c in (has_next, has_outer, relays))
    pl.semaphore_wait(barrier, neighbours)

    @pl.when(has_next)
    def _():
        for copy in sent[:DEPTH]:
            copy.start()

    for copy in own:
        copy.start()

    @pl.loop(0, width // TILE)
    def _(t):
        rows = pl.ds(pl.multiple_of(t * TILE, TILE), TILE)
        offset = iota((TILE, outputs), 0) + t * TILE - STEP * iota((TILE, outputs), 1)
        shifted = offset.astype(F32) + 0.5
        taps = jnp.exp(-(shifted * shifted) / 512.0)
        high, low = split(jnp.where((offset >= -32) & (offset < 32), taps, 0.0))
        weights[rows, 0:outputs] = high
        weights[rows, outputs : 2 * outputs] = low

    pair_copy.wait()
    ramp_copy.wait()

    @pl.loop(0, acqs)
    def _(p):
        cosine, sine = turns(ramp_mem[0, p] * iota((LINES, width), 1), width)
        table[p, 0] = cosine
        table[p, 1] = sine
        line = strip * lines + iota((lines, outputs), 0)
        cosine, sine = turns(ramp_mem[1, p] * line, lines * strip_size)
        line_table[p, 0] = cosine
        line_table[p, 1] = sine

    @pl.when(jnp.logical_not(has_outer))
    def _():
        edges[outer_room] = jnp.zeros(edges.shape[1:], F32)

    slots = [jnp.clip(pair_mem[0, p] - acq * acqs + reach, 0, reach + acqs - 1) for p in range(acqs)]
    half = acqs * 4 * LINES

    def edge_copy(source, room, send, recv, target):
        return pltpu.make_async_remote_copy(
            source, room, edge_send.at[send], recv, device_id=target, device_id_type=MESH
        )

    to_inner = edge_copy(
        looks[0], edges.at[outer_room], 0, edge_recv.at[outer_room], {"strip": inner}
    )
    to_outer = edge_copy(
        looks[1], edges.at[inner_room], 1, edge_recv.at[inner_room], {"strip": outer}
    )
    to_relay = edge_copy(
        looks[0], relayed, 0, relay_recv.at[0], {"acq": acq - place, "strip": relay_out}
    )
    from_relay = edge_copy(
        relayed, edges.at[relay_room], 2, edge_recv.at[relay_room],
        {"acq": acq + from_place, "strip": relay_to},
    )

    def tap_columns(first):
        offset = first + iota((lines, LINES), 1) - iota((lines, LINES), 0)
        value = offset.astype(F32)
        inside = (offset >= -LINES) & (offset <= LINES)
        return jnp.where(inside, jnp.exp(-(value * value) / 32.0), 0.0)

    def azimuth(p, k, blocks, left):
        value = jnp.concatenate(
            [jnp.concatenate([block[p, k], block[p, k + 1]], axis=1) for block in blocks]
        )
        high = value.astype(BF16).astype(F32)
        right = jnp.concatenate([high, value - high, high])
        return jnp.dot(left, right.astype(BF16), preferred_element_type=F32)

    def azimuth_left(firsts):
        taps = jnp.concatenate([tap_columns(first) for first in firsts], axis=1)
        high = taps.astype(BF16).astype(F32)
        return jnp.concatenate([high, high, taps - high], axis=1).astype(BF16)

    early_left = azimuth_left([-LINES, lines, *first_line[:-1]])
    late_left = azimuth_left(first_line[-1:])

    for i, (g, start, count, first_part, last_part) in enumerate(chunks):
        if i == RELAY_AT:

            @pl.when(relays)
            def _():
                to_relay.wait_recv()
                from_relay.start()

        if i + DEPTH < len(chunks):

            @pl.when(has_next)
            def _():
                sent[i].wait_send()
                sent[i + DEPTH].start()

        if i == len(chunks) - 2:
            edge_copy(
                looks[0], edges.at[inner_room], 0, edge_recv.at[inner_room], {"strip": inner}
            ).wait_recv()

            @pl.when(has_outer)
            def _():
                to_inner.wait_recv()

            blocks = [edges.at[0], edges.at[1], *looks[:-1]]
            for p in range(acqs):
                for k in range(0, 4, 2):
                    partial[p, k // 2] = azimuth(p, k, blocks, early_left)

        own[i].wait()

        @pl.when(has_previous)
        def _():
            sent[i].wait_recv()

        piece = pieces[i]
        for t in range(count // TILE):
            here = pl.ds(t * TILE, TILE)
            there = pl.ds(start + t * TILE, TILE)
            for p in range(acqs):
                a, b = piece[slots[p], 0, :, here], piece[slots[p], 1, :, here]
                c, d = piece[reach + p, 0, :, here], piece[reach + p, 1, :, here]
                cosine, sine = table[p, 0, :, there], table[p, 1, :, there]
                x, y = a * c + b * d, b * c - a * d
                value = jnp.concatenate(
                    [x * cosine + y * sine, y * cosine - x * sine, a * a + b * b, c * c + d * d]
                )
                high, low = split(value)
                fields[pl.ds(p * 4 * LINES, 4 * LINES), here] = high
                fields[pl.ds(half + p * 4 * LINES, 4 * LINES), here] = low
        product = jnp.dot(
            fields[:, 0:count], weights[pl.ds(start, count), :], preferred_element_type=F32
        )
        part = (
            product[:half, :outputs] + product[:half, outputs:] + product[half:, :outputs]
        )
        if first_part:
            sums[...] = part
        elif not last_part:
            sums[...] += part
        if last_part:
            whole = part if first_part else sums[...] + part
            whole = whole.reshape(acqs, 4, LINES, outputs)
            for p in range(acqs):
                now = pl.ds(first_line[g], LINES)
                cosine, sine = line_table[p, 0, now, :], line_table[p, 1, now, :]
                x, y = whole[p, 0], whole[p, 1]
                looks[g][p, 0] = x * cosine + y * sine
                looks[g][p, 1] = y * cosine - x * sine
                looks[g][p, 2] = whole[p, 2]
                looks[g][p, 3] = whole[p, 3]
            if g == 0:

                @pl.when(crosses)
                def _():
                    to_relay.start()

                @pl.when(jnp.logical_not(crosses))
                def _():
                    to_inner.start()

            if g == 1:

                @pl.when(has_outer)
                def _():
                    to_outer.start()

    for p in range(acqs):
        summed = []
        for k in range(0, 4, 2):
            value = partial[p, k // 2] + azimuth(p, k, looks[-1:], late_left)
            summed += [value[:, :outputs], value[:, outputs:]]
        scaling = 1.0 / jnp.sqrt(summed[2] * summed[3] + 1e-06)
        out[p, 0] = summed[0] * scaling
        out[p, 1] = summed[1] * scaling

    @pl.when(has_next)
    def _():
        for copy in sent[-DEPTH:]:
            copy.wait_send()

    to_inner.wait_send()

    @pl.when(has_outer)
    def _():
        to_outer.wait_send()

    @pl.when(relays)
    def _():
        from_relay.wait_send()


def body(echoes, pair_list, phase_ramps):
    acqs, _, lines, width = echoes.shape
    groups = lines // LINES
    outputs = width // STEP
    chunks = chunk_list(groups)
    sizes = (acqs, groups, width, lax.axis_size("acq"), lax.axis_size("strip"))
    dma = pltpu.SemaphoreType.DMA
    look = pltpu.VMEM((acqs, 4, LINES, outputs), F32)
    return pl.pallas_call(
        functools.partial(kernel, sizes),
        out_shape=jax.ShapeDtypeStruct((acqs, 2, lines, outputs), F32),
        in_specs=[pl.BlockSpec(memory_space=pl.ANY)] * 3,
        out_specs=pl.BlockSpec(memory_space=pltpu.VMEM),
        scratch_shapes=[
            [pltpu.VMEM((2 * acqs - 1, 2, LINES, c[2]), F32) for c in chunks],
            pltpu.SMEM((2, acqs), I32),
            pltpu.SMEM((2, acqs), I32),
            pltpu.VMEM((width, 2 * outputs), BF16),
            pltpu.VMEM((acqs, 2, LINES, width), F32),
            pltpu.VMEM((acqs, 2, lines, outputs), F32),
            pltpu.VMEM((2 * acqs * 4 * LINES, max(c[2] for c in chunks)), BF16),
            pltpu.VMEM((acqs * 4 * LINES, outputs), F32),
            pltpu.VMEM((acqs, 2, lines, 2 * outputs), F32),
            [look for _ in range(groups)],
            pltpu.VMEM((2, acqs, 4, LINES, outputs), F32),
            look,
            dma((len(chunks),)),
            dma((len(chunks),)),
            dma((len(chunks),)),
            dma((2,)),
            dma((3,)),
            dma((2,)),
            dma((1,)),
        ],
        compiler_params=pltpu.CompilerParams(collective_id=0, has_side_effects=True, vmem_limit_bytes=16 << 20),
    )(*(pltpu.with_memory_space_constraint(v, pltpu.HBM) for v in (echoes, pair_list.T, phase_ramps.T)))


def solution(mesh):
    return jax.shard_map(
        body,
        mesh=mesh,
        in_specs=(P("acq", None, "strip", None), P("acq", None), P("acq", None)),
        out_specs=P("acq", None, "strip", None),
        check_vma=False,
    )
```

```python
import functools
import math

import jax
import jax.numpy as jnp
from jax import lax
from jax.experimental import pallas as pl
from jax.experimental.pallas import tpu as pltpu
from jax.sharding import PartitionSpec as P

MESH = pl.DeviceIdType.MESH
F32, BF16, I32 = jnp.float32, jnp.bfloat16, jnp.int32
LINES = 8
PARTS = (1024, 1024)
LAST_PARTS = (1024, 768, 256)
DEPTH = 3
DETOUR_AT = 2
RELAY_AT = 3
CHIPS = 4
STEP = 16
TILE = 256


def iota(shape, dim):
    return lax.broadcasted_iota(I32, shape, dim)


def split(value):
    high = value.astype(BF16)
    return high, (value - high.astype(F32)).astype(BF16)


def turns(count, whole):
    angle = (count & (whole - 1)).astype(F32) * (2.0 * math.pi / whole)
    return jnp.cos(angle), jnp.sin(angle)


def chunk_list(groups):
    chunks = []
    for g in range(groups):
        parts = LAST_PARTS if g == groups - 1 else PARTS
        start = 0
        for i, count in enumerate(parts):
            chunks.append((g, start, count, i == 0, i == len(parts) - 1))
            start += count
    return chunks


def kernel(
    sizes, echoes, pairs, ramps, out, pieces, pair_mem, ramp_mem, weights, table, line_table, fields,
    sums, partial, looks, edges, relayed, send_sem, recv_sem, own_sem, small_sem, edge_send, edge_recv,
    relay_recv, detour_send, detour_ready,
):
    acqs, groups, width, acq_size, strip_size = sizes
    reach = acqs - 1
    outputs = width // STEP
    lines = groups * LINES
    acq, strip = lax.axis_index("acq"), lax.axis_index("strip")
    has_next, has_previous = acq < acq_size - 1, acq > 0
    place = lax.rem(acq, CHIPS)
    middle, last = strip_size // 2, strip_size - 1

    upper = strip < middle
    inner = jnp.where(upper, strip + 1, strip - 1)
    outer = jnp.where(upper, strip - 1, strip + 1)
    outer_room = jnp.where(upper, 0, 1)
    inner_room = 1 - outer_room
    has_outer = (strip > 0) & (strip < last)
    order = [jnp.where(upper, groups - 1, 0), jnp.where(upper, 0, groups - 1), *range(1, groups - 1)]
    first_line = [pl.multiple_of(g * LINES, LINES) for g in order]

    crosses = ((strip == middle - 1) | (strip == middle)) & (place != 0)
    down_relay = jnp.where(place == 1, middle - 2, jnp.where(place == 2, last, last - 1))
    relay_out = jnp.where(upper, down_relay, last - down_relay)
    relay_in = last - relay_out
    depth = jnp.where(upper, strip, last - strip)
    relays = (place == 0) & (depth < middle - 1)
    from_place = jnp.where(depth == middle - 2, 1, jnp.where(depth == 0, 2, 3))
    relays_down = upper == (from_place == 1)
    relay_from = jnp.where(relays_down, middle - 1, middle)
    relay_to = jnp.where(relays_down, middle, middle - 1)
    relay_room = jnp.where(relays_down, 0, 1)
    chunks = chunk_list(groups)

    long_from = acq_size // 2 - 1
    detour = len(chunks) - 2
    starts_detour, passes_detour = acq == long_from, acq == 0

    barrier = pltpu.get_barrier_semaphore()

    def greet(condition, target):
        @pl.when(condition)
        def _():
            pl.semaphore_signal(barrier, inc=1, device_id=target, device_id_type=MESH)

    greet(has_previous, {"acq": acq - 1})
    greet(jnp.logical_not(crosses), {"strip": inner})
    greet(crosses, {"acq": acq - place, "strip": relay_in})
    greet(has_outer, {"strip": outer})
    greet(starts_detour | (acq == long_from + 1), {"acq": jnp.int32(0)})
    greet(relays, {"acq": acq + from_place, "strip": relay_from})

    pair_copy = pltpu.make_async_copy(pairs, pair_mem, small_sem.at[0])
    ramp_copy = pltpu.make_async_copy(ramps, ramp_mem, small_sem.at[1])
    pair_copy.start()
    ramp_copy.start()

    def region(first, g, start, count):
        return echoes.at[
            pl.ds(first, acqs - first), :, pl.ds(first_line[g], LINES), pl.ds(start, count)
        ]

    own, sent = [], []
    for i, (g, start, count, _, _) in enumerate(chunks):
        own.append(
            pltpu.make_async_copy(
                region(0, g, start, count), pieces[i].at[pl.ds(reach, acqs)], own_sem.at[i]
            )
        )
        sent.append(
            pltpu.make_async_remote_copy(
                pieces[i].at[pl.ds(acqs, reach)], pieces[i].at[pl.ds(0, reach)], send_sem.at[i], recv_sem.at[i],
                device_id={"acq": jnp.where(starts_detour, 0, acq + 1) if i == detour else acq + 1},
                device_id_type=MESH,
            )
        )

    for copy in own:
        copy.start()

    neighbours = 1 + sum(c.astype(I32) for c in (has_next, has_outer, relays))
    neighbours += 2 * passes_detour.astype(I32)
    pl.semaphore_wait(barrier, neighbours)
    for copy in own[:DEPTH]:
        copy.wait()

    @pl.when(passes_detour)
    def _():
        pl.semaphore_signal(
            detour_ready, inc=1, device_id={"acq": jnp.int32(long_from)}, device_id_type=MESH
        )

    @pl.when(has_next)
    def _():
        for copy in sent[:DEPTH]:
            copy.start()

    for copy in own[DEPTH:]:
        copy.wait()

    @pl.loop(0, width // TILE)
    def _(t):
        rows = pl.ds(pl.multiple_of(t * TILE, TILE), TILE)
        offset = iota((TILE, outputs), 0) + t * TILE - STEP * iota((TILE, outputs), 1)
        shifted = offset.astype(F32) + 0.5
        taps = jnp.exp(-(shifted * shifted) / 512.0)
        high, low = split(jnp.where((offset >= -32) & (offset < 32), taps, 0.0))
        weights[rows, 0:outputs] = high
        weights[rows, outputs : 2 * outputs] = low

    pair_copy.wait()
    ramp_copy.wait()

    @pl.loop(0, acqs)
    def _(p):
        cosine, sine = turns(ramp_mem[0, p] * iota((LINES, width), 1), width)
        table[p, 0] = cosine
        table[p, 1] = sine
        line = strip * lines + iota((lines, outputs), 0)
        cosine, sine = turns(ramp_mem[1, p] * line, lines * strip_size)
        line_table[p, 0] = cosine
        line_table[p, 1] = sine

    @pl.when(jnp.logical_not(has_outer))
    def _():
        edges[outer_room] = jnp.zeros(edges.shape[1:], F32)

    detour_on = pltpu.make_async_remote_copy(
        pieces[detour].at[pl.ds(0, reach)], pieces[detour].at[pl.ds(0, reach)],
        detour_send.at[0], recv_sem.at[detour],
        device_id={"acq": jnp.int32(long_from + 1)}, device_id_type=MESH,
    )
    slots = [jnp.clip(pair_mem[0, p] - acq * acqs + reach, 0, reach + acqs - 1) for p in range(acqs)]
    half = acqs * 4 * LINES

    def edge_copy(source, room, send, recv, target):
        return pltpu.make_async_remote_copy(
            source, room, edge_send.at[send], recv, device_id=target, device_id_type=MESH
        )

    to_inner = edge_copy(
        looks[0], edges.at[outer_room], 0, edge_recv.at[outer_room], {"strip": inner}
    )
    to_outer = edge_copy(
        looks[1], edges.at[inner_room], 1, edge_recv.at[inner_room], {"strip": outer}
    )
    to_relay = edge_copy(
        looks[0], relayed, 0, relay_recv.at[0], {"acq": acq - place, "strip": relay_out}
    )
    from_relay = edge_copy(
        relayed, edges.at[relay_room], 2, edge_recv.at[relay_room],
        {"acq": acq + from_place, "strip": relay_to},
    )

    def tap_columns(first):
        offset = first + iota((lines, LINES), 1) - iota((lines, LINES), 0)
        value = offset.astype(F32)
        inside = (offset >= -LINES) & (offset <= LINES)
        return jnp.where(inside, jnp.exp(-(value * value) / 32.0), 0.0)

    def azimuth(p, k, blocks, left):
        value = jnp.concatenate(
            [jnp.concatenate([block[p, k], block[p, k + 1]], axis=1) for block in blocks]
        )
        high = value.astype(BF16).astype(F32)
        right = jnp.concatenate([high, value - high, high])
        return jnp.dot(left, right.astype(BF16), preferred_element_type=F32)

    def azimuth_left(firsts):
        taps = jnp.concatenate([tap_columns(first) for first in firsts], axis=1)
        high = taps.astype(BF16).astype(F32)
        return jnp.concatenate([high, high, taps - high], axis=1).astype(BF16)

    early_left = azimuth_left([-LINES, lines, *first_line[:-1]])
    late_left = azimuth_left(first_line[-1:])

    for i, (g, start, count, first_part, last_part) in enumerate(chunks):
        if i == RELAY_AT:

            @pl.when(relays)
            def _():
                to_relay.wait_recv()
                from_relay.start()

        if i == DETOUR_AT:

            @pl.when(starts_detour)
            def _():
                pl.semaphore_wait(detour_ready, 1)
                sent[detour].start()

        if i + DEPTH < len(chunks):

            @pl.when(has_next)
            def _():
                sent[i].wait_send()

            @pl.when(has_next & jnp.logical_not(starts_detour) if i + DEPTH == detour else has_next)
            def _():
                sent[i + DEPTH].start()

        if i == len(chunks) - 2:
            edge_copy(
                looks[0], edges.at[inner_room], 0, edge_recv.at[inner_room], {"strip": inner}
            ).wait_recv()

            @pl.when(has_outer)
            def _():
                to_inner.wait_recv()

            blocks = [edges.at[0], edges.at[1], *looks[:-1]]
            for p in range(acqs):
                for k in range(0, 4, 2):
                    partial[p, k // 2] = azimuth(p, k, blocks, early_left)

        if i == detour:

            @pl.when(passes_detour)
            def _():
                sent[i].wait_recv()
                detour_on.start()

        @pl.when(has_previous)
        def _():
            sent[i].wait_recv()

        piece = pieces[i]
        for t in range(count // TILE):
            here = pl.ds(t * TILE, TILE)
            there = pl.ds(start + t * TILE, TILE)
            for p in range(acqs):
                a, b = piece[slots[p], 0, :, here], piece[slots[p], 1, :, here]
                c, d = piece[reach + p, 0, :, here], piece[reach + p, 1, :, here]
                cosine, sine = table[p, 0, :, there], table[p, 1, :, there]
                x, y = a * c + b * d, b * c - a * d
                value = jnp.concatenate(
                    [x * cosine + y * sine, y * cosine - x * sine, a * a + b * b, c * c + d * d]
                )
                high, low = split(value)
                fields[pl.ds(p * 4 * LINES, 4 * LINES), here] = high
                fields[pl.ds(half + p * 4 * LINES, 4 * LINES), here] = low
        product = jnp.dot(
            fields[:, 0:count], weights[pl.ds(start, count), :], preferred_element_type=F32
        )
        part = (
            product[:half, :outputs] + product[:half, outputs:] + product[half:, :outputs]
        )
        if first_part:
            sums[...] = part
        elif not last_part:
            sums[...] += part
        if last_part:
            whole = part if first_part else sums[...] + part
            whole = whole.reshape(acqs, 4, LINES, outputs)
            for p in range(acqs):
                now = pl.ds(first_line[g], LINES)
                cosine, sine = line_table[p, 0, now, :], line_table[p, 1, now, :]
                x, y = whole[p, 0], whole[p, 1]
                looks[g][p, 0] = x * cosine + y * sine
                looks[g][p, 1] = y * cosine - x * sine
                looks[g][p, 2] = whole[p, 2]
                looks[g][p, 3] = whole[p, 3]
            if g == 0:

                @pl.when(crosses)
                def _():
                    to_relay.start()

                @pl.when(jnp.logical_not(crosses))
                def _():
                    to_inner.start()

            if g == 1:

                @pl.when(has_outer)
                def _():
                    to_outer.start()

    for p in range(acqs):
        summed = []
        for k in range(0, 4, 2):
            value = partial[p, k // 2] + azimuth(p, k, looks[-1:], late_left)
            summed += [value[:, :outputs], value[:, outputs:]]
        scaling = 1.0 / jnp.sqrt(summed[2] * summed[3] + 1e-06)
        out[p, 0] = summed[0] * scaling
        out[p, 1] = summed[1] * scaling

    @pl.when(has_next)
    def _():
        for copy in sent[-DEPTH:]:
            copy.wait_send()

    @pl.when(passes_detour)
    def _():
        detour_on.wait_send()

    to_inner.wait_send()

    @pl.when(has_outer)
    def _():
        to_outer.wait_send()

    @pl.when(relays)
    def _():
        from_relay.wait_send()


def body(echoes, pair_list, phase_ramps):
    acqs, _, lines, width = echoes.shape
    groups = lines // LINES
    outputs = width // STEP
    chunks = chunk_list(groups)
    sizes = (acqs, groups, width, lax.axis_size("acq"), lax.axis_size("strip"))
    dma = pltpu.SemaphoreType.DMA
    look = pltpu.VMEM((acqs, 4, LINES, outputs), F32)
    return pl.pallas_call(
        functools.partial(kernel, sizes),
        out_shape=jax.ShapeDtypeStruct((acqs, 2, lines, outputs), F32),
        in_specs=[pl.BlockSpec(memory_space=pl.ANY)] * 3,
        out_specs=pl.BlockSpec(memory_space=pltpu.VMEM),
        scratch_shapes=[
            [pltpu.VMEM((2 * acqs - 1, 2, LINES, c[2]), F32) for c in chunks],
            pltpu.SMEM((2, acqs), I32),
            pltpu.SMEM((2, acqs), I32),
            pltpu.VMEM((width, 2 * outputs), BF16),
            pltpu.VMEM((acqs, 2, LINES, width), F32),
            pltpu.VMEM((acqs, 2, lines, outputs), F32),
            pltpu.VMEM((2 * acqs * 4 * LINES, max(c[2] for c in chunks)), BF16),
            pltpu.VMEM((acqs * 4 * LINES, outputs), F32),
            pltpu.VMEM((acqs, 2, lines, 2 * outputs), F32),
            [look for _ in range(groups)],
            pltpu.VMEM((2, acqs, 4, LINES, outputs), F32),
            look,
            dma((len(chunks),)),
            dma((len(chunks),)),
            dma((len(chunks),)),
            dma((2,)),
            dma((3,)),
            dma((2,)),
            dma((1,)),
            dma((1,)),
            pltpu.SemaphoreType.REGULAR,
        ],
        compiler_params=pltpu.CompilerParams(collective_id=0, has_side_effects=True, vmem_limit_bytes=16 << 20),
    )(*(pltpu.with_memory_space_constraint(v, pltpu.HBM) for v in (echoes, pair_list.T, phase_ramps.T)))


def solution(mesh):
    return jax.shard_map(
        body,
        mesh=mesh,
        in_specs=(P("acq", None, "strip", None), P("acq", None), P("acq", None)),
        out_specs=P("acq", None, "strip", None),
        check_vma=False,
    )
```

```python
import functools
import math

import jax
import jax.numpy as jnp
from jax import lax
from jax.experimental import pallas as pl
from jax.experimental.pallas import tpu as pltpu
from jax.sharding import PartitionSpec as P

MESH = pl.DeviceIdType.MESH
F32, BF16, I32 = jnp.float32, jnp.bfloat16, jnp.int32
LINES = 8
PARTS = (2048,)
LAST_PARTS = (1024, 768, 256)
DEPTH = 3
DETOUR_AT = 1
RELAY_AT = 1
CHIPS = 4
STEP = 16
TILE = 256


def iota(shape, dim):
    return lax.broadcasted_iota(I32, shape, dim)


def split(value):
    high = value.astype(BF16)
    return high, (value - high.astype(F32)).astype(BF16)


def turns(count, whole):
    angle = (count & (whole - 1)).astype(F32) * (2.0 * math.pi / whole)
    return jnp.cos(angle), jnp.sin(angle)


def chunk_list(groups):
    chunks = []
    for g in range(groups):
        parts = LAST_PARTS if g == groups - 1 else PARTS
        start = 0
        for i, count in enumerate(parts):
            chunks.append((g, start, count, i == 0, i == len(parts) - 1))
            start += count
    return chunks


def kernel(
    sizes, echoes, pairs, ramps, out, pieces, pair_mem, ramp_mem, weights, table, line_table, fields,
    sums, partial, looks, edges, relayed, send_sem, recv_sem, own_sem, edge_send, edge_recv,
    relay_recv, detour_send, detour_ready,
):
    acqs, groups, width, acq_size, strip_size = sizes
    reach = acqs - 1
    outputs = width // STEP
    lines = groups * LINES
    acq, strip = lax.axis_index("acq"), lax.axis_index("strip")
    has_next, has_previous = acq < acq_size - 1, acq > 0
    place = lax.rem(acq, CHIPS)
    middle, last = strip_size // 2, strip_size - 1

    upper = strip < middle
    inner = jnp.where(upper, strip + 1, strip - 1)
    outer = jnp.where(upper, strip - 1, strip + 1)
    outer_room = jnp.where(upper, 0, 1)
    inner_room = 1 - outer_room
    has_outer = (strip > 0) & (strip < last)
    order = [jnp.where(upper, groups - 1, 0), jnp.where(upper, 0, groups - 1), *range(1, groups - 1)]
    first_line = [pl.multiple_of(g * LINES, LINES) for g in order]

    crosses = ((strip == middle - 1) | (strip == middle)) & (place != 0)
    down_relay = jnp.where(place == 1, middle - 2, jnp.where(place == 2, last, last - 1))
    relay_out = jnp.where(upper, down_relay, last - down_relay)
    relay_in = last - relay_out
    depth = jnp.where(upper, strip, last - strip)
    relays = (place == 0) & (depth < middle - 1)
    from_place = jnp.where(depth == middle - 2, 1, jnp.where(depth == 0, 2, 3))
    relays_down = upper == (from_place == 1)
    relay_from = jnp.where(relays_down, middle - 1, middle)
    relay_to = jnp.where(relays_down, middle, middle - 1)
    relay_room = jnp.where(relays_down, 0, 1)
    chunks = chunk_list(groups)

    long_from = acq_size // 2 - 1
    detour = len(chunks) - 2
    starts_detour, passes_detour = acq == long_from, acq == 0

    barrier = pltpu.get_barrier_semaphore()

    def greet(condition, target):
        @pl.when(condition)
        def _():
            pl.semaphore_signal(barrier, inc=1, device_id=target, device_id_type=MESH)

    greet(has_previous, {"acq": acq - 1})
    greet(jnp.logical_not(crosses), {"strip": inner})
    greet(crosses, {"acq": acq - place, "strip": relay_in})
    greet(has_outer, {"strip": outer})
    greet(starts_detour | (acq == long_from + 1), {"acq": jnp.int32(0)})
    greet(relays, {"acq": acq + from_place, "strip": relay_from})

    pair_copy = pltpu.make_async_copy(pairs, pair_mem, edge_send.at[0])
    ramp_copy = pltpu.make_async_copy(ramps, ramp_mem, edge_send.at[1])
    pair_copy.start()
    ramp_copy.start()

    def region(first, g, start, count):
        return echoes.at[
            pl.ds(first, acqs - first), :, pl.ds(first_line[g], LINES), pl.ds(start, count)
        ]

    own, sent = [], []
    for i, (g, start, count, _, _) in enumerate(chunks):
        own.append(
            pltpu.make_async_copy(
                region(0, g, start, count), pieces[i].at[pl.ds(reach, acqs)], own_sem.at[i % DEPTH]
            )
        )
        sent.append(
            pltpu.make_async_remote_copy(
                pieces[i].at[pl.ds(acqs, reach)], pieces[i].at[pl.ds(0, reach)],
                detour_send.at[0] if i == detour else send_sem.at[i % DEPTH], recv_sem.at[i],
                device_id={"acq": jnp.where(starts_detour, 0, acq + 1) if i == detour else acq + 1},
                device_id_type=MESH,
            )
        )

    for copy in own[:DEPTH]:
        copy.start()

    neighbours = 1 + sum(c.astype(I32) for c in (has_next, has_outer, relays))
    neighbours += 2 * passes_detour.astype(I32)
    pl.semaphore_wait(barrier, neighbours)

    @pl.when(passes_detour)
    def _():
        pl.semaphore_signal(
            detour_ready, inc=1, device_id={"acq": jnp.int32(long_from)}, device_id_type=MESH
        )

    for i in range(DEPTH):
        own[i].wait()

        @pl.when(has_next)
        def _():
            sent[i].start()

        if i + DEPTH < len(chunks):
            own[i + DEPTH].start()

    @pl.loop(0, width // TILE)
    def _(t):
        rows = pl.ds(pl.multiple_of(t * TILE, TILE), TILE)
        offset = iota((TILE, outputs), 0) + t * TILE - STEP * iota((TILE, outputs), 1)
        shifted = offset.astype(F32) + 0.5
        taps = jnp.exp(-(shifted * shifted) / 512.0)
        high, low = split(jnp.where((offset >= -32) & (offset < 32), taps, 0.0))
        weights[rows, 0:outputs] = high
        weights[rows, outputs : 2 * outputs] = low

    pair_copy.wait()
    ramp_copy.wait()

    @pl.loop(0, acqs)
    def _(p):
        cosine, sine = turns(ramp_mem[0, p] * iota((LINES, width), 1), width)
        table[p, 0] = cosine
        table[p, 1] = sine
        line = strip * lines + iota((lines, outputs), 0)
        cosine, sine = turns(ramp_mem[1, p] * line, lines * strip_size)
        line_table[p, 0] = cosine
        line_table[p, 1] = sine

    @pl.when(jnp.logical_not(has_outer))
    def _():
        edges[outer_room] = jnp.zeros(edges.shape[1:], F32)

    detour_on = pltpu.make_async_remote_copy(
        pieces[detour].at[pl.ds(0, reach)], pieces[detour].at[pl.ds(0, reach)],
        detour_send.at[1], recv_sem.at[detour],
        device_id={"acq": jnp.int32(long_from + 1)}, device_id_type=MESH,
    )
    slots = [jnp.clip(pair_mem[0, p] - acq * acqs + reach, 0, reach + acqs - 1) for p in range(acqs)]
    half = acqs * 4 * LINES

    def edge_copy(source, room, send, recv, target):
        return pltpu.make_async_remote_copy(
            source, room, edge_send.at[send], recv, device_id=target, device_id_type=MESH
        )

    to_inner = edge_copy(
        looks[0], edges.at[outer_room], 0, edge_recv.at[outer_room], {"strip": inner}
    )
    to_outer = edge_copy(
        looks[1], edges.at[inner_room], 1, edge_recv.at[inner_room], {"strip": outer}
    )
    to_relay = edge_copy(
        looks[0], relayed, 0, relay_recv.at[0], {"acq": acq - place, "strip": relay_out}
    )
    from_relay = edge_copy(
        relayed, edges.at[relay_room], 2, edge_recv.at[relay_room],
        {"acq": acq + from_place, "strip": relay_to},
    )

    def tap_columns(first):
        offset = first + iota((lines, LINES), 1) - iota((lines, LINES), 0)
        value = offset.astype(F32)
        inside = (offset >= -LINES) & (offset <= LINES)
        return jnp.where(inside, jnp.exp(-(value * value) / 32.0), 0.0)

    def azimuth(p, k, blocks, left):
        value = jnp.concatenate(
            [jnp.concatenate([block[p, k], block[p, k + 1]], axis=1) for block in blocks]
        )
        high = value.astype(BF16).astype(F32)
        right = jnp.concatenate([high, value - high, high])
        return jnp.dot(left, right.astype(BF16), preferred_element_type=F32)

    def azimuth_left(firsts):
        taps = jnp.concatenate([tap_columns(first) for first in firsts], axis=1)
        high = taps.astype(BF16).astype(F32)
        return jnp.concatenate([high, high, taps - high], axis=1).astype(BF16)

    early_left = azimuth_left([-LINES, lines, *first_line[:-1]])
    late_left = azimuth_left(first_line[-1:])

    for i, (g, start, count, first_part, last_part) in enumerate(chunks):
        if i == RELAY_AT:

            @pl.when(relays)
            def _():
                to_relay.wait_recv()
                from_relay.start()

        if i + DEPTH < len(chunks):
            own[i + DEPTH].wait()

        if i == DETOUR_AT:

            @pl.when(starts_detour)
            def _():
                pl.semaphore_wait(detour_ready, 1)
                sent[detour].start()

        if i + DEPTH < len(chunks):
            @pl.when(has_next)
            def _():
                sent[i].wait_send()

            @pl.when(has_next & jnp.logical_not(starts_detour) if i + DEPTH == detour else has_next)
            def _():
                sent[i + DEPTH].start()

        if i == len(chunks) - 2:
            edge_copy(
                looks[0], edges.at[inner_room], 0, edge_recv.at[inner_room], {"strip": inner}
            ).wait_recv()

            @pl.when(has_outer)
            def _():
                to_inner.wait_recv()

            blocks = [edges.at[0], edges.at[1], *looks[:-1]]
            for p in range(acqs):
                for k in range(0, 4, 2):
                    partial[p, k // 2] = azimuth(p, k, blocks, early_left)

        if i == detour:

            @pl.when(passes_detour)
            def _():
                sent[i].wait_recv()
                detour_on.start()

        @pl.when(has_previous)
        def _():
            sent[i].wait_recv()

        piece = pieces[i]
        for t in range(count // TILE):
            here = pl.ds(t * TILE, TILE)
            there = pl.ds(start + t * TILE, TILE)
            for p in range(acqs):
                a, b = piece[slots[p], 0, :, here], piece[slots[p], 1, :, here]
                c, d = piece[reach + p, 0, :, here], piece[reach + p, 1, :, here]
                cosine, sine = table[p, 0, :, there], table[p, 1, :, there]
                x, y = a * c + b * d, b * c - a * d
                value = jnp.concatenate(
                    [x * cosine + y * sine, y * cosine - x * sine, a * a + b * b, c * c + d * d]
                )
                high, low = split(value)
                fields[pl.ds(p * 4 * LINES, 4 * LINES), here] = high
                fields[pl.ds(half + p * 4 * LINES, 4 * LINES), here] = low
        product = jnp.dot(
            fields[:, 0:count], weights[pl.ds(start, count), :], preferred_element_type=F32
        )
        part = (
            product[:half, :outputs] + product[:half, outputs:] + product[half:, :outputs]
        )
        if first_part:
            sums[...] = part
        elif not last_part:
            sums[...] += part
        if last_part:
            whole = part if first_part else sums[...] + part
            whole = whole.reshape(acqs, 4, LINES, outputs)
            for p in range(acqs):
                now = pl.ds(first_line[g], LINES)
                cosine, sine = line_table[p, 0, now, :], line_table[p, 1, now, :]
                x, y = whole[p, 0], whole[p, 1]
                looks[g][p, 0] = x * cosine + y * sine
                looks[g][p, 1] = y * cosine - x * sine
                looks[g][p, 2] = whole[p, 2]
                looks[g][p, 3] = whole[p, 3]
            if g == 0:

                @pl.when(crosses)
                def _():
                    to_relay.start()

                @pl.when(jnp.logical_not(crosses))
                def _():
                    to_inner.start()

            if g == 1:

                @pl.when(has_outer)
                def _():
                    to_outer.start()

    for p in range(acqs):
        summed = []
        for k in range(0, 4, 2):
            value = partial[p, k // 2] + azimuth(p, k, looks[-1:], late_left)
            summed += [value[:, :outputs], value[:, outputs:]]
        scaling = 1.0 / jnp.sqrt(summed[2] * summed[3] + 1e-06)
        out[p, 0] = summed[0] * scaling
        out[p, 1] = summed[1] * scaling

    @pl.when(has_next)
    def _():
        for copy in sent[-DEPTH:]:
            copy.wait_send()

    @pl.when(passes_detour)
    def _():
        detour_on.wait_send()

    to_inner.wait_send()

    @pl.when(has_outer)
    def _():
        to_outer.wait_send()

    @pl.when(relays)
    def _():
        from_relay.wait_send()


def body(echoes, pair_list, phase_ramps):
    acqs, _, lines, width = echoes.shape
    groups = lines // LINES
    outputs = width // STEP
    chunks = chunk_list(groups)
    sizes = (acqs, groups, width, lax.axis_size("acq"), lax.axis_size("strip"))
    dma = pltpu.SemaphoreType.DMA
    look = pltpu.VMEM((acqs, 4, LINES, outputs), F32)
    return pl.pallas_call(
        functools.partial(kernel, sizes),
        out_shape=jax.ShapeDtypeStruct((acqs, 2, lines, outputs), F32),
        in_specs=[pl.BlockSpec(memory_space=pl.ANY)] * 3,
        out_specs=pl.BlockSpec(memory_space=pltpu.VMEM),
        scratch_shapes=[
            [pltpu.VMEM((2 * acqs - 1, 2, LINES, c[2]), F32) for c in chunks],
            pltpu.SMEM((2, acqs), I32),
            pltpu.SMEM((2, acqs), I32),
            pltpu.VMEM((width, 2 * outputs), BF16),
            pltpu.VMEM((acqs, 2, LINES, width), F32),
            pltpu.VMEM((acqs, 2, lines, outputs), F32),
            pltpu.VMEM((2 * acqs * 4 * LINES, max(c[2] for c in chunks)), BF16),
            pltpu.VMEM((acqs * 4 * LINES, outputs), F32),
            pltpu.VMEM((acqs, 2, lines, 2 * outputs), F32),
            [look for _ in range(groups)],
            pltpu.VMEM((2, acqs, 4, LINES, outputs), F32),
            look,
            dma((DEPTH,)),
            dma((len(chunks),)),
            dma((DEPTH,)),
            dma((3,)),
            dma((2,)),
            dma((1,)),
            dma((2,)),
            pltpu.SemaphoreType.REGULAR,
        ],
        compiler_params=pltpu.CompilerParams(collective_id=0, has_side_effects=True, vmem_limit_bytes=16 << 20),
    )(*(pltpu.with_memory_space_constraint(v, pltpu.HBM) for v in (echoes, pair_list.T, phase_ramps.T)))


def solution(mesh):
    return jax.shard_map(
        body,
        mesh=mesh,
        in_specs=(P("acq", None, "strip", None), P("acq", None), P("acq", None)),
        out_specs=P("acq", None, "strip", None),
        check_vma=False,
    )
```

```python
import functools
import math

import jax
import jax.numpy as jnp
from jax import lax
from jax.experimental import pallas as pl
from jax.experimental.pallas import tpu as pltpu
from jax.sharding import PartitionSpec as P

MESH = pl.DeviceIdType.MESH
F32, BF16, I32 = jnp.float32, jnp.bfloat16, jnp.int32
LINES = 8
PARTS = (2048,)
LAST_PARTS = (1024, 768, 256)
DEPTH = 3
DETOUR_AT = 1
RELAY_AT = 1
CHIPS = 4
STEP = 16
TILE = 256


def iota(shape, dim):
    return lax.broadcasted_iota(I32, shape, dim)


def split(value):
    high = value.astype(BF16)
    return high, (value - high.astype(F32)).astype(BF16)


def turns(count, whole):
    angle = (count & (whole - 1)).astype(F32) * (2.0 * math.pi / whole)
    return jnp.cos(angle), jnp.sin(angle)


def chunk_list(groups):
    chunks = []
    for g in range(groups):
        parts = LAST_PARTS if g == groups - 1 else PARTS
        start = 0
        for i, count in enumerate(parts):
            chunks.append((g, start, count, i == 0, i == len(parts) - 1))
            start += count
    return chunks


def kernel(
    sizes, echoes, pairs, ramps, out, pieces, pair_mem, ramp_mem, weights, table, line_table, fields,
    sums, partial, looks, edges, relayed, send_sem, recv_sem, own_sem, edge_send, edge_recv,
    relay_recv, detour_send, detour_ready,
    relay_ready,
):
    acqs, groups, width, acq_size, strip_size = sizes
    reach = acqs - 1
    outputs = width // STEP
    lines = groups * LINES
    acq, strip = lax.axis_index("acq"), lax.axis_index("strip")
    has_next, has_previous = acq < acq_size - 1, acq > 0
    place = lax.rem(acq, CHIPS)
    middle, last = strip_size // 2, strip_size - 1

    upper = strip < middle
    inner = jnp.where(upper, strip + 1, strip - 1)
    outer = jnp.where(upper, strip - 1, strip + 1)
    outer_room = jnp.where(upper, 0, 1)
    inner_room = 1 - outer_room
    has_outer = (strip > 0) & (strip < last)
    order = [jnp.where(upper, groups - 1, 0), jnp.where(upper, 0, groups - 1), *range(1, groups - 1)]
    first_line = [pl.multiple_of(g * LINES, LINES) for g in order]

    crosses = ((strip == middle - 1) | (strip == middle)) & (place != 0)
    down_relay = jnp.where(place == 1, middle - 2, jnp.where(place == 2, last, last - 1))
    relay_out = jnp.where(upper, down_relay, last - down_relay)
    relay_in = last - relay_out
    depth = jnp.where(upper, strip, last - strip)
    relays = (place == 0) & (depth < middle - 1)
    from_place = jnp.where(depth == middle - 2, 1, jnp.where(depth == 0, 2, 3))
    relays_down = upper == (from_place == 1)
    relay_from = jnp.where(relays_down, middle - 1, middle)
    relay_to = jnp.where(relays_down, middle, middle - 1)
    relay_room = jnp.where(relays_down, 0, 1)
    chunks = chunk_list(groups)

    long_from = acq_size // 2 - 1
    detour = len(chunks) - 2
    starts_detour, passes_detour = acq == long_from, acq == 0

    barrier = pltpu.get_barrier_semaphore()

    def greet(condition, target):
        @pl.when(condition)
        def _():
            pl.semaphore_signal(barrier, inc=1, device_id=target, device_id_type=MESH)

    greet(has_previous, {"acq": acq - 1})
    greet(jnp.logical_not(crosses), {"strip": inner})
    greet(crosses, {"acq": acq - place, "strip": relay_in})
    greet(has_outer, {"strip": outer})
    greet(starts_detour | (acq == long_from + 1), {"acq": jnp.int32(0)})
    greet(crosses, {"acq": acq - place, "strip": relay_out})

    pair_copy = pltpu.make_async_copy(pairs, pair_mem, edge_send.at[0])
    ramp_copy = pltpu.make_async_copy(ramps, ramp_mem, edge_send.at[1])
    pair_copy.start()
    ramp_copy.start()

    def region(first, g, start, count):
        return echoes.at[
            pl.ds(first, acqs - first), :, pl.ds(first_line[g], LINES), pl.ds(start, count)
        ]

    own, sent = [], []
    for i, (g, start, count, _, _) in enumerate(chunks):
        own.append(
            pltpu.make_async_copy(
                region(0, g, start, count), pieces[i].at[pl.ds(reach, acqs)], own_sem.at[i % DEPTH]
            )
        )
        sent.append(
            pltpu.make_async_remote_copy(
                pieces[i].at[pl.ds(acqs, reach)], pieces[i].at[pl.ds(0, reach)],
                detour_send.at[0] if i == detour else send_sem.at[i % DEPTH], recv_sem.at[i],
                device_id={"acq": jnp.where(starts_detour, 0, acq + 1) if i == detour else acq + 1},
                device_id_type=MESH,
            )
        )

    for copy in own[:DEPTH]:
        copy.start()

    waits = (has_next, has_outer, jnp.logical_not(crosses), relays, relays)
    neighbours = sum(c.astype(I32) for c in waits)
    neighbours += 2 * passes_detour.astype(I32)
    pl.semaphore_wait(barrier, neighbours)

    for i in range(DEPTH):
        own[i].wait()

        @pl.when(has_next)
        def _():
            sent[i].start()

        if i + DEPTH < len(chunks):
            own[i + DEPTH].start()

    @pl.when(relays)
    def _():
        pl.semaphore_signal(
            relay_ready, inc=1, device_id={"acq": acq + from_place, "strip": relay_from},
            device_id_type=MESH,
        )

    @pl.when(passes_detour)
    def _():
        pl.semaphore_signal(
            detour_ready, inc=1, device_id={"acq": jnp.int32(long_from)}, device_id_type=MESH
        )

    @pl.loop(0, width // TILE)
    def _(t):
        rows = pl.ds(pl.multiple_of(t * TILE, TILE), TILE)
        offset = iota((TILE, outputs), 0) + t * TILE - STEP * iota((TILE, outputs), 1)
        shifted = offset.astype(F32) + 0.5
        taps = jnp.exp(-(shifted * shifted) / 512.0)
        high, low = split(jnp.where((offset >= -32) & (offset < 32), taps, 0.0))
        weights[rows, 0:outputs] = high
        weights[rows, outputs : 2 * outputs] = low

    pair_copy.wait()
    ramp_copy.wait()

    @pl.loop(0, acqs)
    def _(p):
        cosine, sine = turns(ramp_mem[0, p] * iota((LINES, width), 1), width)
        table[p, 0] = cosine
        table[p, 1] = sine
        line = strip * lines + iota((lines, outputs), 0)
        cosine, sine = turns(ramp_mem[1, p] * line, lines * strip_size)
        line_table[p, 0] = cosine
        line_table[p, 1] = sine

    @pl.when(jnp.logical_not(has_outer))
    def _():
        edges[outer_room] = jnp.zeros(edges.shape[1:], F32)

    detour_on = pltpu.make_async_remote_copy(
        pieces[detour].at[pl.ds(0, reach)], pieces[detour].at[pl.ds(0, reach)],
        detour_send.at[1], recv_sem.at[detour],
        device_id={"acq": jnp.int32(long_from + 1)}, device_id_type=MESH,
    )
    slots = [jnp.clip(pair_mem[0, p] - acq * acqs + reach, 0, reach + acqs - 1) for p in range(acqs)]
    half = acqs * 4 * LINES

    def edge_copy(source, room, send, recv, target):
        return pltpu.make_async_remote_copy(
            source, room, edge_send.at[send], recv, device_id=target, device_id_type=MESH
        )

    to_inner = edge_copy(
        looks[0], edges.at[outer_room], 0, edge_recv.at[outer_room], {"strip": inner}
    )
    to_outer = edge_copy(
        looks[1], edges.at[inner_room], 1, edge_recv.at[inner_room], {"strip": outer}
    )
    to_relay = edge_copy(
        looks[0], relayed, 0, relay_recv.at[0], {"acq": acq - place, "strip": relay_out}
    )
    from_relay = edge_copy(
        relayed, edges.at[relay_room], 2, edge_recv.at[relay_room],
        {"acq": acq + from_place, "strip": relay_to},
    )

    def tap_columns(first):
        offset = first + iota((lines, LINES), 1) - iota((lines, LINES), 0)
        value = offset.astype(F32)
        inside = (offset >= -LINES) & (offset <= LINES)
        return jnp.where(inside, jnp.exp(-(value * value) / 32.0), 0.0)

    def azimuth(p, k, blocks, left):
        value = jnp.concatenate(
            [jnp.concatenate([block[p, k], block[p, k + 1]], axis=1) for block in blocks]
        )
        high = value.astype(BF16).astype(F32)
        right = jnp.concatenate([high, value - high, high])
        return jnp.dot(left, right.astype(BF16), preferred_element_type=F32)

    def azimuth_left(firsts):
        taps = jnp.concatenate([tap_columns(first) for first in firsts], axis=1)
        high = taps.astype(BF16).astype(F32)
        return jnp.concatenate([high, high, taps - high], axis=1).astype(BF16)

    early_left = azimuth_left([-LINES, lines, *first_line[:-1]])
    late_left = azimuth_left(first_line[-1:])

    for i, (g, start, count, first_part, last_part) in enumerate(chunks):
        if i == RELAY_AT:

            @pl.when(relays)
            def _():
                to_relay.wait_recv()
                from_relay.start()

        if i + DEPTH < len(chunks):
            own[i + DEPTH].wait()

        if i == DETOUR_AT:

            @pl.when(starts_detour)
            def _():
                pl.semaphore_wait(detour_ready, 1)
                sent[detour].start()

        if i + DEPTH < len(chunks):
            @pl.when(has_next)
            def _():
                sent[i].wait_send()

            @pl.when(has_next & jnp.logical_not(starts_detour) if i + DEPTH == detour else has_next)
            def _():
                sent[i + DEPTH].start()

        if i == len(chunks) - 2:
            edge_copy(
                looks[0], edges.at[inner_room], 0, edge_recv.at[inner_room], {"strip": inner}
            ).wait_recv()

            @pl.when(has_outer)
            def _():
                to_inner.wait_recv()

            blocks = [edges.at[0], edges.at[1], *looks[:-1]]
            for p in range(acqs):
                for k in range(0, 4, 2):
                    partial[p, k // 2] = azimuth(p, k, blocks, early_left)

        if i == detour:

            @pl.when(passes_detour)
            def _():
                sent[i].wait_recv()
                detour_on.start()

        @pl.when(has_previous)
        def _():
            sent[i].wait_recv()

        piece = pieces[i]
        for t in range(count // TILE):
            here = pl.ds(t * TILE, TILE)
            there = pl.ds(start + t * TILE, TILE)
            for p in range(acqs):
                a, b = piece[slots[p], 0, :, here], piece[slots[p], 1, :, here]
                c, d = piece[reach + p, 0, :, here], piece[reach + p, 1, :, here]
                cosine, sine = table[p, 0, :, there], table[p, 1, :, there]
                x, y = a * c + b * d, b * c - a * d
                value = jnp.concatenate(
                    [x * cosine + y * sine, y * cosine - x * sine, a * a + b * b, c * c + d * d]
                )
                high, low = split(value)
                fields[pl.ds(p * 4 * LINES, 4 * LINES), here] = high
                fields[pl.ds(half + p * 4 * LINES, 4 * LINES), here] = low
        product = jnp.dot(
            fields[:, 0:count], weights[pl.ds(start, count), :], preferred_element_type=F32
        )
        part = (
            product[:half, :outputs] + product[:half, outputs:] + product[half:, :outputs]
        )
        if first_part:
            sums[...] = part
        elif not last_part:
            sums[...] += part
        if last_part:
            whole = part if first_part else sums[...] + part
            whole = whole.reshape(acqs, 4, LINES, outputs)
            for p in range(acqs):
                now = pl.ds(first_line[g], LINES)
                cosine, sine = line_table[p, 0, now, :], line_table[p, 1, now, :]
                x, y = whole[p, 0], whole[p, 1]
                looks[g][p, 0] = x * cosine + y * sine
                looks[g][p, 1] = y * cosine - x * sine
                looks[g][p, 2] = whole[p, 2]
                looks[g][p, 3] = whole[p, 3]
            if g == 0:

                @pl.when(crosses)
                def _():
                    pl.semaphore_wait(relay_ready, 1)
                    to_relay.start()

                @pl.when(jnp.logical_not(crosses))
                def _():
                    to_inner.start()

            if g == 1:

                @pl.when(has_outer)
                def _():
                    to_outer.start()

    for p in range(acqs):
        summed = []
        for k in range(0, 4, 2):
            value = partial[p, k // 2] + azimuth(p, k, looks[-1:], late_left)
            summed += [value[:, :outputs], value[:, outputs:]]
        scaling = 1.0 / jnp.sqrt(summed[2] * summed[3] + 1e-06)
        out[p, 0] = summed[0] * scaling
        out[p, 1] = summed[1] * scaling

    @pl.when(has_next)
    def _():
        for copy in sent[-DEPTH:]:
            copy.wait_send()

    @pl.when(passes_detour)
    def _():
        detour_on.wait_send()

    to_inner.wait_send()

    @pl.when(has_outer)
    def _():
        to_outer.wait_send()

    @pl.when(relays)
    def _():
        from_relay.wait_send()


def body(echoes, pair_list, phase_ramps):
    acqs, _, lines, width = echoes.shape
    groups = lines // LINES
    outputs = width // STEP
    chunks = chunk_list(groups)
    sizes = (acqs, groups, width, lax.axis_size("acq"), lax.axis_size("strip"))
    dma = pltpu.SemaphoreType.DMA
    look = pltpu.VMEM((acqs, 4, LINES, outputs), F32)
    return pl.pallas_call(
        functools.partial(kernel, sizes),
        out_shape=jax.ShapeDtypeStruct((acqs, 2, lines, outputs), F32),
        in_specs=[pl.BlockSpec(memory_space=pl.ANY)] * 3,
        out_specs=pl.BlockSpec(memory_space=pltpu.VMEM),
        scratch_shapes=[
            [pltpu.VMEM((2 * acqs - 1, 2, LINES, c[2]), F32) for c in chunks],
            pltpu.SMEM((2, acqs), I32),
            pltpu.SMEM((2, acqs), I32),
            pltpu.VMEM((width, 2 * outputs), BF16),
            pltpu.VMEM((acqs, 2, LINES, width), F32),
            pltpu.VMEM((acqs, 2, lines, outputs), F32),
            pltpu.VMEM((2 * acqs * 4 * LINES, max(c[2] for c in chunks)), BF16),
            pltpu.VMEM((acqs * 4 * LINES, outputs), F32),
            pltpu.VMEM((acqs, 2, lines, 2 * outputs), F32),
            [look for _ in range(groups)],
            pltpu.VMEM((2, acqs, 4, LINES, outputs), F32),
            look,
            dma((DEPTH,)),
            dma((len(chunks),)),
            dma((DEPTH,)),
            dma((3,)),
            dma((2,)),
            dma((1,)),
            dma((2,)),
            pltpu.SemaphoreType.REGULAR,
            pltpu.SemaphoreType.REGULAR,
        ],
        compiler_params=pltpu.CompilerParams(collective_id=0, has_side_effects=True, vmem_limit_bytes=16 << 20),
    )(*(pltpu.with_memory_space_constraint(v, pltpu.HBM) for v in (echoes, pair_list.T, phase_ramps.T)))


def solution(mesh):
    return jax.shard_map(
        body,
        mesh=mesh,
        in_specs=(P("acq", None, "strip", None), P("acq", None), P("acq", None)),
        out_specs=P("acq", None, "strip", None),
        check_vma=False,
    )
```

```python
import functools
import math

import jax
import jax.numpy as jnp
from jax import lax
from jax.experimental import pallas as pl
from jax.experimental.pallas import tpu as pltpu
from jax.sharding import PartitionSpec as P

MESH = pl.DeviceIdType.MESH
F32, BF16, I32 = jnp.float32, jnp.bfloat16, jnp.int32
LINES = 8
PARTS = (2048,)
LAST_PARTS = (1024, 768, 256)
DEPTH = 3
DETOUR_AT = 1
PASS_AT = 3
RELAY_AT = 1
CHIPS = 4
STEP = 16
TILE = 256


def iota(shape, dim):
    return lax.broadcasted_iota(I32, shape, dim)


def split(value):
    high = value.astype(BF16)
    return high, (value - high.astype(F32)).astype(BF16)


def turns(count, whole):
    angle = (count & (whole - 1)).astype(F32) * (2.0 * math.pi / whole)
    return jnp.cos(angle), jnp.sin(angle)


def chunk_list(groups):
    chunks = []
    for g in range(groups):
        parts = LAST_PARTS if g == groups - 1 else PARTS
        start = 0
        for i, count in enumerate(parts):
            chunks.append((g, start, count, i == 0, i == len(parts) - 1))
            start += count
    return chunks


def kernel(
    sizes, echoes, pairs, ramps, out, pieces, pair_mem, ramp_mem, weights, table, line_table, fields,
    sums, partial, looks, edges, relayed, send_sem, recv_sem, own_sem, edge_send, edge_recv,
    relay_recv, detour_send, detour_ready,
    relay_ready,
):
    acqs, groups, width, acq_size, strip_size = sizes
    reach = acqs - 1
    outputs = width // STEP
    lines = groups * LINES
    acq, strip = lax.axis_index("acq"), lax.axis_index("strip")
    has_next, has_previous = acq < acq_size - 1, acq > 0
    place = lax.rem(acq, CHIPS)
    middle, last = strip_size // 2, strip_size - 1

    upper = strip < middle
    inner = jnp.where(upper, strip + 1, strip - 1)
    outer = jnp.where(upper, strip - 1, strip + 1)
    outer_room = jnp.where(upper, 0, 1)
    inner_room = 1 - outer_room
    has_outer = (strip > 0) & (strip < last)
    order = [jnp.where(upper, groups - 1, 0), jnp.where(upper, 0, groups - 1), *range(1, groups - 1)]
    first_line = [pl.multiple_of(g * LINES, LINES) for g in order]

    crosses = ((strip == middle - 1) | (strip == middle)) & (place != 0)
    down_relay = jnp.where(place == 1, middle - 2, jnp.where(place == 2, last, last - 1))
    relay_out = jnp.where(upper, down_relay, last - down_relay)
    relay_in = last - relay_out
    depth = jnp.where(upper, strip, last - strip)
    relays = (place == 0) & (depth < middle - 1)
    from_place = jnp.where(depth == middle - 2, 1, jnp.where(depth == 0, 2, 3))
    relays_down = upper == (from_place == 1)
    relay_from = jnp.where(relays_down, middle - 1, middle)
    relay_to = jnp.where(relays_down, middle, middle - 1)
    relay_room = jnp.where(relays_down, 0, 1)
    chunks = chunk_list(groups)

    long_from = acq_size // 2 - 1
    detour = len(chunks) - 2
    starts_detour, passes_detour = acq == long_from, acq == 0

    barrier = pltpu.get_barrier_semaphore()

    def greet(condition, target):
        @pl.when(condition)
        def _():
            pl.semaphore_signal(barrier, inc=1, device_id=target, device_id_type=MESH)

    greet(has_previous, {"acq": acq - 1})
    greet(jnp.logical_not(crosses), {"strip": inner})
    greet(crosses, {"acq": acq - place, "strip": relay_in})
    greet(has_outer, {"strip": outer})
    greet(starts_detour | (acq == long_from + 1), {"acq": jnp.int32(0)})
    greet(crosses, {"acq": acq - place, "strip": relay_out})

    pair_copy = pltpu.make_async_copy(pairs, pair_mem, edge_send.at[0])
    ramp_copy = pltpu.make_async_copy(ramps, ramp_mem, edge_send.at[1])
    pair_copy.start()
    ramp_copy.start()

    def region(first, g, start, count):
        return echoes.at[
            pl.ds(first, acqs - first), :, pl.ds(first_line[g], LINES), pl.ds(start, count)
        ]

    own, sent = [], []
    for i, (g, start, count, _, _) in enumerate(chunks):
        own.append(
            pltpu.make_async_copy(
                region(0, g, start, count), pieces[i].at[pl.ds(reach, acqs)], own_sem.at[i % DEPTH]
            )
        )
        sent.append(
            pltpu.make_async_remote_copy(
                pieces[i].at[pl.ds(acqs, reach)], pieces[i].at[pl.ds(0, reach)],
                detour_send.at[0] if i == detour else send_sem.at[i % DEPTH], recv_sem.at[i],
                device_id={"acq": jnp.where(starts_detour, 0, acq + 1) if i == detour else acq + 1},
                device_id_type=MESH,
            )
        )

    for copy in own[:DEPTH]:
        copy.start()

    waits = (has_next, has_outer, jnp.logical_not(crosses), relays, relays)
    neighbours = sum(c.astype(I32) for c in waits)
    neighbours += 2 * passes_detour.astype(I32)
    pl.semaphore_wait(barrier, neighbours)

    for i in range(DEPTH):
        own[i].wait()

        @pl.when(has_next)
        def _():
            sent[i].start()

        if i + DEPTH < len(chunks):
            own[i + DEPTH].start()

    @pl.when(relays)
    def _():
        pl.semaphore_signal(
            relay_ready, inc=1, device_id={"acq": acq + from_place, "strip": relay_from},
            device_id_type=MESH,
        )

    @pl.when(passes_detour)
    def _():
        pl.semaphore_signal(
            detour_ready, inc=1, device_id={"acq": jnp.int32(long_from)}, device_id_type=MESH
        )

    @pl.loop(0, width // TILE)
    def _(t):
        rows = pl.ds(pl.multiple_of(t * TILE, TILE), TILE)
        offset = iota((TILE, outputs), 0) + t * TILE - STEP * iota((TILE, outputs), 1)
        shifted = offset.astype(F32) + 0.5
        taps = jnp.exp(-(shifted * shifted) / 512.0)
        high, low = split(jnp.where((offset >= -32) & (offset < 32), taps, 0.0))
        weights[rows, 0:outputs] = high
        weights[rows, outputs : 2 * outputs] = low

    pair_copy.wait()
    ramp_copy.wait()

    @pl.loop(0, acqs)
    def _(p):
        cosine, sine = turns(ramp_mem[0, p] * iota((LINES, width), 1), width)
        table[p, 0] = cosine
        table[p, 1] = sine
        line = strip * lines + iota((lines, outputs), 0)
        cosine, sine = turns(ramp_mem[1, p] * line, lines * strip_size)
        line_table[p, 0] = cosine
        line_table[p, 1] = sine

    @pl.when(jnp.logical_not(has_outer))
    def _():
        edges[outer_room] = jnp.zeros(edges.shape[1:], F32)

    detour_on = pltpu.make_async_remote_copy(
        pieces[detour].at[pl.ds(0, reach)], pieces[detour].at[pl.ds(0, reach)],
        detour_send.at[1], recv_sem.at[detour],
        device_id={"acq": jnp.int32(long_from + 1)}, device_id_type=MESH,
    )
    slots = [jnp.clip(pair_mem[0, p] - acq * acqs + reach, 0, reach + acqs - 1) for p in range(acqs)]
    half = acqs * 4 * LINES

    def edge_copy(source, room, send, recv, target):
        return pltpu.make_async_remote_copy(
            source, room, edge_send.at[send], recv, device_id=target, device_id_type=MESH
        )

    to_inner = edge_copy(
        looks[0], edges.at[outer_room], 0, edge_recv.at[outer_room], {"strip": inner}
    )
    to_outer = edge_copy(
        looks[1], edges.at[inner_room], 1, edge_recv.at[inner_room], {"strip": outer}
    )
    to_relay = edge_copy(
        looks[0], relayed, 0, relay_recv.at[0], {"acq": acq - place, "strip": relay_out}
    )
    from_relay = edge_copy(
        relayed, edges.at[relay_room], 2, edge_recv.at[relay_room],
        {"acq": acq + from_place, "strip": relay_to},
    )

    def tap_columns(first):
        offset = first + iota((lines, LINES), 1) - iota((lines, LINES), 0)
        value = offset.astype(F32)
        inside = (offset >= -LINES) & (offset <= LINES)
        return jnp.where(inside, jnp.exp(-(value * value) / 32.0), 0.0)

    def azimuth(p, k, blocks, left):
        value = jnp.concatenate(
            [jnp.concatenate([block[p, k], block[p, k + 1]], axis=1) for block in blocks]
        )
        high = value.astype(BF16).astype(F32)
        right = jnp.concatenate([high, value - high, high])
        return jnp.dot(left, right.astype(BF16), preferred_element_type=F32)

    def azimuth_left(firsts):
        taps = jnp.concatenate([tap_columns(first) for first in firsts], axis=1)
        high = taps.astype(BF16).astype(F32)
        return jnp.concatenate([high, high, taps - high], axis=1).astype(BF16)

    early_left = azimuth_left([-LINES, lines, *first_line[:-1]])
    late_left = azimuth_left(first_line[-1:])

    for i, (g, start, count, first_part, last_part) in enumerate(chunks):
        if i == PASS_AT:

            @pl.when(passes_detour)
            def _():
                sent[detour].wait_recv()
                detour_on.start()

        if i == RELAY_AT:

            @pl.when(relays)
            def _():
                to_relay.wait_recv()
                from_relay.start()

        if i + DEPTH < len(chunks):
            own[i + DEPTH].wait()

        if i == DETOUR_AT:

            @pl.when(starts_detour)
            def _():
                pl.semaphore_wait(detour_ready, 1)
                sent[detour].start()

        if i + DEPTH < len(chunks):
            @pl.when(has_next)
            def _():
                sent[i].wait_send()

            @pl.when(has_next & jnp.logical_not(starts_detour) if i + DEPTH == detour else has_next)
            def _():
                sent[i + DEPTH].start()

        if i == len(chunks) - 2:
            edge_copy(
                looks[0], edges.at[inner_room], 0, edge_recv.at[inner_room], {"strip": inner}
            ).wait_recv()

            @pl.when(has_outer)
            def _():
                to_inner.wait_recv()

            blocks = [edges.at[0], edges.at[1], *looks[:-1]]
            for p in range(acqs):
                for k in range(0, 4, 2):
                    partial[p, k // 2] = azimuth(p, k, blocks, early_left)

        @pl.when(has_previous)
        def _():
            sent[i].wait_recv()

        piece = pieces[i]
        for t in range(count // TILE):
            here = pl.ds(t * TILE, TILE)
            there = pl.ds(start + t * TILE, TILE)
            for p in range(acqs):
                a, b = piece[slots[p], 0, :, here], piece[slots[p], 1, :, here]
                c, d = piece[reach + p, 0, :, here], piece[reach + p, 1, :, here]
                cosine, sine = table[p, 0, :, there], table[p, 1, :, there]
                x, y = a * c + b * d, b * c - a * d
                value = jnp.concatenate(
                    [x * cosine + y * sine, y * cosine - x * sine, a * a + b * b, c * c + d * d]
                )
                high, low = split(value)
                fields[pl.ds(p * 4 * LINES, 4 * LINES), here] = high
                fields[pl.ds(half + p * 4 * LINES, 4 * LINES), here] = low
        product = jnp.dot(
            fields[:, 0:count], weights[pl.ds(start, count), :], preferred_element_type=F32
        )
        part = (
            product[:half, :outputs] + product[:half, outputs:] + product[half:, :outputs]
        )
        if first_part:
            sums[...] = part
        elif not last_part:
            sums[...] += part
        if last_part:
            whole = part if first_part else sums[...] + part
            whole = whole.reshape(acqs, 4, LINES, outputs)
            for p in range(acqs):
                now = pl.ds(first_line[g], LINES)
                cosine, sine = line_table[p, 0, now, :], line_table[p, 1, now, :]
                x, y = whole[p, 0], whole[p, 1]
                looks[g][p, 0] = x * cosine + y * sine
                looks[g][p, 1] = y * cosine - x * sine
                looks[g][p, 2] = whole[p, 2]
                looks[g][p, 3] = whole[p, 3]
            if g == 0:

                @pl.when(crosses)
                def _():
                    pl.semaphore_wait(relay_ready, 1)
                    to_relay.start()

                @pl.when(jnp.logical_not(crosses))
                def _():
                    to_inner.start()

            if g == 1:

                @pl.when(has_outer)
                def _():
                    to_outer.start()

    for p in range(acqs):
        summed = []
        for k in range(0, 4, 2):
            value = partial[p, k // 2] + azimuth(p, k, looks[-1:], late_left)
            summed += [value[:, :outputs], value[:, outputs:]]
        scaling = 1.0 / jnp.sqrt(summed[2] * summed[3] + 1e-06)
        out[p, 0] = summed[0] * scaling
        out[p, 1] = summed[1] * scaling

    @pl.when(has_next)
    def _():
        for copy in sent[-DEPTH:]:
            copy.wait_send()

    @pl.when(passes_detour)
    def _():
        detour_on.wait_send()

    to_inner.wait_send()

    @pl.when(has_outer)
    def _():
        to_outer.wait_send()

    @pl.when(relays)
    def _():
        from_relay.wait_send()


def body(echoes, pair_list, phase_ramps):
    acqs, _, lines, width = echoes.shape
    groups = lines // LINES
    outputs = width // STEP
    chunks = chunk_list(groups)
    sizes = (acqs, groups, width, lax.axis_size("acq"), lax.axis_size("strip"))
    dma = pltpu.SemaphoreType.DMA
    look = pltpu.VMEM((acqs, 4, LINES, outputs), F32)
    return pl.pallas_call(
        functools.partial(kernel, sizes),
        out_shape=jax.ShapeDtypeStruct((acqs, 2, lines, outputs), F32),
        in_specs=[pl.BlockSpec(memory_space=pl.ANY)] * 3,
        out_specs=pl.BlockSpec(memory_space=pltpu.VMEM),
        scratch_shapes=[
            [pltpu.VMEM((2 * acqs - 1, 2, LINES, c[2]), F32) for c in chunks],
            pltpu.SMEM((2, acqs), I32),
            pltpu.SMEM((2, acqs), I32),
            pltpu.VMEM((width, 2 * outputs), BF16),
            pltpu.VMEM((acqs, 2, LINES, width), F32),
            pltpu.VMEM((acqs, 2, lines, outputs), F32),
            pltpu.VMEM((2 * acqs * 4 * LINES, max(c[2] for c in chunks)), BF16),
            pltpu.VMEM((acqs * 4 * LINES, outputs), F32),
            pltpu.VMEM((acqs, 2, lines, 2 * outputs), F32),
            [look for _ in range(groups)],
            pltpu.VMEM((2, acqs, 4, LINES, outputs), F32),
            look,
            dma((DEPTH,)),
            dma((len(chunks),)),
            dma((DEPTH,)),
            dma((3,)),
            dma((2,)),
            dma((1,)),
            dma((2,)),
            pltpu.SemaphoreType.REGULAR,
            pltpu.SemaphoreType.REGULAR,
        ],
        compiler_params=pltpu.CompilerParams(collective_id=0, has_side_effects=True, vmem_limit_bytes=16 << 20),
    )(*(pltpu.with_memory_space_constraint(v, pltpu.HBM) for v in (echoes, pair_list.T, phase_ramps.T)))


def solution(mesh):
    return jax.shard_map(
        body,
        mesh=mesh,
        in_specs=(P("acq", None, "strip", None), P("acq", None), P("acq", None)),
        out_specs=P("acq", None, "strip", None),
        check_vma=False,
    )
```

```python
import functools
import math

import jax
import jax.numpy as jnp
from jax import lax
from jax.experimental import pallas as pl
from jax.experimental.pallas import tpu as pltpu
from jax.sharding import PartitionSpec as P

MESH = pl.DeviceIdType.MESH
F32, BF16, I32 = jnp.float32, jnp.bfloat16, jnp.int32
LINES = 8
PARTS = (2048,)
LAST_PARTS = (1024, 768, 256)
DEPTH = 3
DETOUR_AT = 1
PASS_AT = 3
RELAY_AT = 1
CHIPS = 4
STEP = 16
TILE = 256


def iota(shape, dim):
    return lax.broadcasted_iota(I32, shape, dim)


def split(value):
    high = value.astype(BF16)
    return high, (value - high.astype(F32)).astype(BF16)


def turns(count, whole):
    angle = (count & (whole - 1)).astype(F32) * (2.0 * math.pi / whole)
    return jnp.cos(angle), jnp.sin(angle)


def chunk_list(groups):
    chunks = []
    for g in range(groups):
        parts = LAST_PARTS if g == groups - 1 else PARTS
        start = 0
        for i, count in enumerate(parts):
            chunks.append((g, start, count, i == 0, i == len(parts) - 1))
            start += count
    return chunks


def kernel(
    sizes, echoes, pairs, ramps, out, pieces, pair_mem, ramp_mem, weights, table, line_table, fields,
    sums, partial, looks, edges, relayed, send_sem, recv_sem, own_sem, edge_send, edge_recv,
    relay_recv, detour_send, detour_ready,
    relay_ready,
):
    acqs, groups, width, acq_size, strip_size = sizes
    reach = acqs - 1
    outputs = width // STEP
    lines = groups * LINES
    acq, strip = lax.axis_index("acq"), lax.axis_index("strip")
    has_next, has_previous = acq < acq_size - 1, acq > 0
    place = lax.rem(acq, CHIPS)
    middle, last = strip_size // 2, strip_size - 1

    upper = strip < middle
    inner = jnp.where(upper, strip + 1, strip - 1)
    outer = jnp.where(upper, strip - 1, strip + 1)
    outer_room = jnp.where(upper, 0, 1)
    inner_room = 1 - outer_room
    has_outer = (strip > 0) & (strip < last)
    order = [jnp.where(upper, groups - 1, 0), jnp.where(upper, 0, groups - 1), *range(1, groups - 1)]
    first_line = [pl.multiple_of(g * LINES, LINES) for g in order]

    crosses = ((strip == middle - 1) | (strip == middle)) & (place != 0)
    down_relay = jnp.where(place == 1, middle - 2, jnp.where(place == 2, last, last - 1))
    relay_out = jnp.where(upper, down_relay, last - down_relay)
    relay_in = last - relay_out
    depth = jnp.where(upper, strip, last - strip)
    relays = (place == 0) & (depth < middle - 1)
    from_place = jnp.where(depth == middle - 2, 1, jnp.where(depth == 0, 2, 3))
    relays_down = upper == (from_place == 1)
    relay_from = jnp.where(relays_down, middle - 1, middle)
    relay_to = jnp.where(relays_down, middle, middle - 1)
    relay_room = jnp.where(relays_down, 0, 1)
    chunks = chunk_list(groups)

    long_from = acq_size // 2 - 1
    detour = len(chunks) - 2
    starts_detour, passes_detour = acq == long_from, acq == 0

    barrier = pltpu.get_barrier_semaphore()

    def greet(condition, target):
        @pl.when(condition)
        def _():
            pl.semaphore_signal(barrier, inc=1, device_id=target, device_id_type=MESH)

    greet(has_previous, {"acq": acq - 1})
    greet(jnp.logical_not(crosses), {"strip": inner})
    greet(crosses, {"acq": acq - place, "strip": relay_in})
    greet(has_outer, {"strip": outer})
    greet(starts_detour | (acq == long_from + 1), {"acq": jnp.int32(0)})
    greet(crosses, {"acq": acq - place, "strip": relay_out})

    pair_copy = pltpu.make_async_copy(pairs, pair_mem, edge_send.at[0])
    ramp_copy = pltpu.make_async_copy(ramps, ramp_mem, edge_send.at[1])
    pair_copy.start()
    ramp_copy.start()

    def region(first, g, start, count):
        return echoes.at[
            pl.ds(first, acqs - first), :, pl.ds(first_line[g], LINES), pl.ds(start, count)
        ]

    own, sent = [], []
    for i, (g, start, count, _, _) in enumerate(chunks):
        own.append(
            pltpu.make_async_copy(
                region(0, g, start, count), pieces[i].at[pl.ds(reach, acqs)], own_sem.at[i % DEPTH]
            )
        )
        sent.append(
            pltpu.make_async_remote_copy(
                pieces[i].at[pl.ds(acqs, reach)], pieces[i].at[pl.ds(0, reach)],
                detour_send.at[0] if i == detour else send_sem.at[i % DEPTH], recv_sem.at[i],
                device_id={"acq": jnp.where(starts_detour, 0, acq + 1) if i == detour else acq + 1},
                device_id_type=MESH,
            )
        )

    for copy in own[:DEPTH]:
        copy.start()

    waits = (has_next, has_outer, jnp.logical_not(crosses), relays, relays)
    neighbours = sum(c.astype(I32) for c in waits)
    neighbours += 2 * passes_detour.astype(I32)
    pl.semaphore_wait(barrier, neighbours)

    for i in range(DEPTH):
        own[i].wait()

        @pl.when(has_next)
        def _():
            sent[i].start()

        if i + DEPTH < len(chunks):
            own[i + DEPTH].start()

    @pl.when(relays)
    def _():
        pl.semaphore_signal(
            relay_ready, inc=1, device_id={"acq": acq + from_place, "strip": relay_from},
            device_id_type=MESH,
        )

    @pl.when(passes_detour)
    def _():
        pl.semaphore_signal(
            detour_ready, inc=1, device_id={"acq": jnp.int32(long_from)}, device_id_type=MESH
        )

    @pl.loop(0, width // TILE)
    def _(t):
        rows = pl.ds(pl.multiple_of(t * TILE, TILE), TILE)
        offset = iota((TILE, outputs), 0) + t * TILE - STEP * iota((TILE, outputs), 1)
        shifted = offset.astype(F32) + 0.5
        taps = jnp.exp(-(shifted * shifted) / 512.0)
        high, low = split(jnp.where((offset >= -32) & (offset < 32), taps, 0.0))
        weights[rows, 0:outputs] = high
        weights[rows, outputs : 2 * outputs] = low

    pair_copy.wait()
    ramp_copy.wait()

    @pl.loop(0, acqs)
    def _(p):
        cosine, sine = turns(ramp_mem[0, p] * iota((LINES, width), 1), width)
        table[p, 0] = cosine
        table[p, 1] = sine
        line = strip * lines + iota((lines, outputs), 0)
        cosine, sine = turns(ramp_mem[1, p] * line, lines * strip_size)
        line_table[p, 0] = cosine
        line_table[p, 1] = sine

    @pl.when(jnp.logical_not(has_outer))
    def _():
        edges[outer_room] = jnp.zeros(edges.shape[1:], F32)

    detour_on = pltpu.make_async_remote_copy(
        pieces[detour].at[pl.ds(0, reach)], pieces[detour].at[pl.ds(0, reach)],
        own_sem.at[0], recv_sem.at[detour],
        device_id={"acq": jnp.int32(long_from + 1)}, device_id_type=MESH,
    )
    slots = [jnp.clip(pair_mem[0, p] - acq * acqs + reach, 0, reach + acqs - 1) for p in range(acqs)]
    half = acqs * 4 * LINES

    def edge_copy(source, room, send, recv, target):
        return pltpu.make_async_remote_copy(
            source, room, edge_send.at[send], recv, device_id=target, device_id_type=MESH
        )

    to_inner = edge_copy(
        looks[0], edges.at[outer_room], 0, edge_recv.at[outer_room], {"strip": inner}
    )
    to_outer = edge_copy(
        looks[1], edges.at[inner_room], 1, edge_recv.at[inner_room], {"strip": outer}
    )
    to_relay = edge_copy(
        looks[0], relayed, 0, relay_recv.at[0], {"acq": acq - place, "strip": relay_out}
    )
    from_relay = edge_copy(
        relayed, edges.at[relay_room], 2, edge_recv.at[relay_room],
        {"acq": acq + from_place, "strip": relay_to},
    )

    def tap_columns(first):
        offset = first + iota((lines, LINES), 1) - iota((lines, LINES), 0)
        value = offset.astype(F32)
        inside = (offset >= -LINES) & (offset <= LINES)
        return jnp.where(inside, jnp.exp(-(value * value) / 32.0), 0.0)

    def azimuth(p, k, blocks, left):
        value = jnp.concatenate(
            [jnp.concatenate([block[p, k], block[p, k + 1]], axis=1) for block in blocks]
        )
        high = value.astype(BF16).astype(F32)
        right = jnp.concatenate([high, value - high, high])
        return jnp.dot(left, right.astype(BF16), preferred_element_type=F32)

    def azimuth_left(firsts):
        taps = jnp.concatenate([tap_columns(first) for first in firsts], axis=1)
        high = taps.astype(BF16).astype(F32)
        return jnp.concatenate([high, high, taps - high], axis=1).astype(BF16)

    early_left = azimuth_left([-LINES, lines, *first_line[:-1]])
    late_left = azimuth_left(first_line[-1:])

    for i, (g, start, count, first_part, last_part) in enumerate(chunks):
        if i == PASS_AT:

            @pl.when(passes_detour)
            def _():
                sent[detour].wait_recv()
                detour_on.start()

        if i == RELAY_AT:

            @pl.when(relays)
            def _():
                to_relay.wait_recv()
                from_relay.start()

        if i + DEPTH < len(chunks):
            own[i + DEPTH].wait()

        if i == DETOUR_AT:

            @pl.when(starts_detour)
            def _():
                pl.semaphore_wait(detour_ready, 1)
                sent[detour].start()

        if i + DEPTH < len(chunks):
            @pl.when(has_next)
            def _():
                sent[i].wait_send()

            @pl.when(has_next & jnp.logical_not(starts_detour) if i + DEPTH == detour else has_next)
            def _():
                sent[i + DEPTH].start()

        if i == len(chunks) - 2:
            edge_copy(
                looks[0], edges.at[inner_room], 0, edge_recv.at[inner_room], {"strip": inner}
            ).wait_recv()

            @pl.when(has_outer)
            def _():
                to_inner.wait_recv()

            blocks = [edges.at[0], edges.at[1], *looks[:-1]]
            for p in range(acqs):
                for k in range(0, 4, 2):
                    partial[p, k // 2] = azimuth(p, k, blocks, early_left)

        @pl.when(has_previous)
        def _():
            sent[i].wait_recv()

        piece = pieces[i]
        for t in range(count // TILE):
            here = pl.ds(t * TILE, TILE)
            there = pl.ds(start + t * TILE, TILE)
            for p in range(acqs):
                a, b = piece[slots[p], 0, :, here], piece[slots[p], 1, :, here]
                c, d = piece[reach + p, 0, :, here], piece[reach + p, 1, :, here]
                cosine, sine = table[p, 0, :, there], table[p, 1, :, there]
                x, y = a * c + b * d, b * c - a * d
                value = jnp.concatenate(
                    [x * cosine + y * sine, y * cosine - x * sine, a * a + b * b, c * c + d * d]
                )
                high, low = split(value)
                fields[pl.ds(p * 4 * LINES, 4 * LINES), here] = high
                fields[pl.ds(half + p * 4 * LINES, 4 * LINES), here] = low
        product = jnp.dot(
            fields[:, 0:count], weights[pl.ds(start, count), :], preferred_element_type=F32
        )
        part = (
            product[:half, :outputs] + product[:half, outputs:] + product[half:, :outputs]
        )
        if first_part:
            sums[...] = part
        elif not last_part:
            sums[...] += part
        if last_part:
            whole = part if first_part else sums[...] + part
            whole = whole.reshape(acqs, 4, LINES, outputs)
            for p in range(acqs):
                now = pl.ds(first_line[g], LINES)
                cosine, sine = line_table[p, 0, now, :], line_table[p, 1, now, :]
                x, y = whole[p, 0], whole[p, 1]
                looks[g][p, 0] = x * cosine + y * sine
                looks[g][p, 1] = y * cosine - x * sine
                looks[g][p, 2] = whole[p, 2]
                looks[g][p, 3] = whole[p, 3]
            if g == 0:

                @pl.when(crosses)
                def _():
                    pl.semaphore_wait(relay_ready, 1)
                    to_relay.start()

                @pl.when(jnp.logical_not(crosses))
                def _():
                    to_inner.start()

            if g == 1:

                @pl.when(has_outer)
                def _():
                    to_outer.start()

    for p in range(acqs):
        summed = []
        for k in range(0, 4, 2):
            value = partial[p, k // 2] + azimuth(p, k, looks[-1:], late_left)
            summed += [value[:, :outputs], value[:, outputs:]]
        scaling = lax.rsqrt(summed[2] * summed[3] + 1e-06)
        out[p, 0] = summed[0] * scaling
        out[p, 1] = summed[1] * scaling

    @pl.when(has_next)
    def _():
        for copy in sent[-DEPTH:]:
            copy.wait_send()

    @pl.when(passes_detour)
    def _():
        detour_on.wait_send()

    to_inner.wait_send()

    @pl.when(has_outer)
    def _():
        to_outer.wait_send()

    @pl.when(relays)
    def _():
        from_relay.wait_send()


def body(echoes, pair_list, phase_ramps):
    acqs, _, lines, width = echoes.shape
    groups = lines // LINES
    outputs = width // STEP
    chunks = chunk_list(groups)
    sizes = (acqs, groups, width, lax.axis_size("acq"), lax.axis_size("strip"))
    dma = pltpu.SemaphoreType.DMA
    look = pltpu.VMEM((acqs, 4, LINES, outputs), F32)
    return pl.pallas_call(
        functools.partial(kernel, sizes),
        out_shape=jax.ShapeDtypeStruct((acqs, 2, lines, outputs), F32),
        in_specs=[pl.BlockSpec(memory_space=pl.ANY)] * 3,
        out_specs=pl.BlockSpec(memory_space=pltpu.VMEM),
        scratch_shapes=[
            [pltpu.VMEM((2 * acqs - 1, 2, LINES, c[2]), F32) for c in chunks],
            pltpu.SMEM((2, acqs), I32),
            pltpu.SMEM((2, acqs), I32),
            pltpu.VMEM((width, 2 * outputs), BF16),
            pltpu.VMEM((acqs, 2, LINES, width), F32),
            pltpu.VMEM((acqs, 2, lines, outputs), F32),
            pltpu.VMEM((2 * acqs * 4 * LINES, max(c[2] for c in chunks)), BF16),
            pltpu.VMEM((acqs * 4 * LINES, outputs), F32),
            pltpu.VMEM((acqs, 2, lines, 2 * outputs), F32),
            [look for _ in range(groups)],
            pltpu.VMEM((2, acqs, 4, LINES, outputs), F32),
            look,
            dma((DEPTH,)),
            dma((len(chunks),)),
            dma((DEPTH,)),
            dma((3,)),
            dma((2,)),
            dma((1,)),
            dma((1,)),
            pltpu.SemaphoreType.REGULAR,
            pltpu.SemaphoreType.REGULAR,
        ],
        compiler_params=pltpu.CompilerParams(collective_id=0, has_side_effects=True, vmem_limit_bytes=16 << 20),
    )(*(pltpu.with_memory_space_constraint(v, pltpu.HBM) for v in (echoes, pair_list.T, phase_ramps.T)))


def solution(mesh):
    return jax.shard_map(
        body,
        mesh=mesh,
        in_specs=(P("acq", None, "strip", None), P("acq", None), P("acq", None)),
        out_specs=P("acq", None, "strip", None),
        check_vma=False,
    )
```

```python
import functools
import math

import jax
import jax.numpy as jnp
from jax import lax
from jax.experimental import pallas as pl
from jax.experimental.pallas import tpu as pltpu
from jax.sharding import PartitionSpec as P

MESH = pl.DeviceIdType.MESH
F32, BF16, I32 = jnp.float32, jnp.bfloat16, jnp.int32
LINES = 8
PARTS = (2048,)
LAST_PARTS = (1024, 768, 256)
DEPTH = 3
DETOUR_AT = 1
PASS_AT = 3
RELAY_AT = 1
CHIPS = 4
STEP = 16
TILE = 256


def iota(shape, dim):
    return lax.broadcasted_iota(I32, shape, dim)


def split(value):
    high = value.astype(BF16)
    return high, (value - high.astype(F32)).astype(BF16)


def turns(count, whole):
    angle = (count & (whole - 1)).astype(F32) * (2.0 * math.pi / whole)
    return jnp.cos(angle), jnp.sin(angle)


def chunk_list(groups):
    chunks = []
    for g in range(groups):
        parts = LAST_PARTS if g == groups - 1 else PARTS
        start = 0
        for i, count in enumerate(parts):
            chunks.append((g, start, count, i == 0, i == len(parts) - 1))
            start += count
    return chunks


def kernel(
    sizes, echoes, pairs, ramps, out, pieces, pair_mem, ramp_mem, weights, table, line_table, fields,
    sums, partial, looks, edges, relayed, send_sem, recv_sem, own_sem, edge_send, edge_recv,
    relay_recv, detour_send, detour_ready,
    relay_ready,
):
    acqs, groups, width, acq_size, strip_size = sizes
    reach = acqs - 1
    outputs = width // STEP
    lines = groups * LINES
    acq, strip = lax.axis_index("acq"), lax.axis_index("strip")
    has_next, has_previous = acq < acq_size - 1, acq > 0
    place = lax.rem(acq, CHIPS)
    middle, last = strip_size // 2, strip_size - 1

    upper = strip < middle
    inner = jnp.where(upper, strip + 1, strip - 1)
    outer = jnp.where(upper, strip - 1, strip + 1)
    outer_room = jnp.where(upper, 0, 1)
    inner_room = 1 - outer_room
    has_outer = (strip > 0) & (strip < last)
    order = [jnp.where(upper, groups - 1, 0), jnp.where(upper, 0, groups - 1), *range(1, groups - 1)]
    first_line = [pl.multiple_of(g * LINES, LINES) for g in order]

    crosses = ((strip == middle - 1) | (strip == middle)) & (place != 0)
    down_relay = jnp.where(place == 1, middle - 2, jnp.where(place == 2, last, last - 1))
    relay_out = jnp.where(upper, down_relay, last - down_relay)
    relay_in = last - relay_out
    depth = jnp.where(upper, strip, last - strip)
    relays = (place == 0) & (depth < middle - 1)
    from_place = jnp.where(depth == middle - 2, 1, jnp.where(depth == 0, 2, 3))
    relays_down = upper == (from_place == 1)
    relay_from = jnp.where(relays_down, middle - 1, middle)
    relay_to = jnp.where(relays_down, middle, middle - 1)
    relay_room = jnp.where(relays_down, 0, 1)
    chunks = chunk_list(groups)

    long_from = acq_size // 2 - 1
    detour = len(chunks) - 2
    starts_detour, passes_detour = acq == long_from, acq == 0

    barrier = pltpu.get_barrier_semaphore()

    def greet(condition, target):
        @pl.when(condition)
        def _():
            pl.semaphore_signal(barrier, inc=1, device_id=target, device_id_type=MESH)

    greet(has_previous, {"acq": acq - 1})
    greet(jnp.logical_not(crosses), {"strip": inner})
    greet(crosses, {"acq": acq - place, "strip": relay_in})
    greet(has_outer, {"strip": outer})
    greet(starts_detour | (acq == long_from + 1), {"acq": jnp.int32(0)})
    greet(crosses, {"acq": acq - place, "strip": relay_out})

    pair_copy = pltpu.make_async_copy(pairs, pair_mem, edge_send.at[0])
    ramp_copy = pltpu.make_async_copy(ramps, ramp_mem, edge_send.at[1])
    pair_copy.start()
    ramp_copy.start()

    def region(first, g, start, count):
        return echoes.at[
            pl.ds(first, acqs - first), :, pl.ds(first_line[g], LINES), pl.ds(start, count)
        ]

    own, sent = [], []
    for i, (g, start, count, _, _) in enumerate(chunks):
        own.append(
            pltpu.make_async_copy(
                region(0, g, start, count), pieces[i].at[pl.ds(reach, acqs)], own_sem.at[i % DEPTH]
            )
        )
        sent.append(
            pltpu.make_async_remote_copy(
                pieces[i].at[pl.ds(acqs, reach)], pieces[i].at[pl.ds(0, reach)],
                detour_send.at[0] if i == detour else send_sem.at[i % DEPTH], recv_sem.at[i],
                device_id={"acq": jnp.where(starts_detour, 0, acq + 1) if i == detour else acq + 1},
                device_id_type=MESH,
            )
        )

    for copy in own[:DEPTH]:
        copy.start()

    waits = (has_next, has_outer, jnp.logical_not(crosses), relays, relays)
    neighbours = sum(c.astype(I32) for c in waits)
    neighbours += 2 * passes_detour.astype(I32)
    pl.semaphore_wait(barrier, neighbours)

    for i in range(DEPTH):
        own[i].wait()

        @pl.when(has_next)
        def _():
            sent[i].start()

        if i + DEPTH < len(chunks):
            own[i + DEPTH].start()

    @pl.when(relays)
    def _():
        pl.semaphore_signal(
            relay_ready, inc=1, device_id={"acq": acq + from_place, "strip": relay_from},
            device_id_type=MESH,
        )

    @pl.when(passes_detour)
    def _():
        pl.semaphore_signal(
            detour_ready, inc=1, device_id={"acq": jnp.int32(long_from)}, device_id_type=MESH
        )

    @pl.loop(0, width // TILE)
    def _(t):
        rows = pl.ds(pl.multiple_of(t * TILE, TILE), TILE)
        offset = iota((TILE, outputs), 0) + t * TILE - STEP * iota((TILE, outputs), 1)
        shifted = offset.astype(F32) + 0.5
        taps = jnp.exp(-(shifted * shifted) / 512.0)
        high, low = split(jnp.where((offset >= -32) & (offset < 32), taps, 0.0))
        weights[rows, 0:outputs] = high
        weights[rows, outputs : 2 * outputs] = low

    pair_copy.wait()
    ramp_copy.wait()

    @pl.loop(0, acqs)
    def _(p):
        cosine, sine = turns(ramp_mem[0, p] * iota((LINES, width), 1), width)
        table[p, 0] = cosine
        table[p, 1] = sine
        line = strip * lines + iota((lines, outputs), 0)
        cosine, sine = turns(ramp_mem[1, p] * line, lines * strip_size)
        line_table[p, 0] = cosine
        line_table[p, 1] = sine

    @pl.when(jnp.logical_not(has_outer))
    def _():
        edges[outer_room] = jnp.zeros(edges.shape[1:], F32)

    detour_on = pltpu.make_async_remote_copy(
        pieces[detour].at[pl.ds(0, reach)], pieces[detour].at[pl.ds(0, reach)],
        own_sem.at[0], recv_sem.at[detour],
        device_id={"acq": jnp.int32(long_from + 1)}, device_id_type=MESH,
    )
    slots = [jnp.clip(pair_mem[0, p] - acq * acqs + reach, 0, reach + acqs - 1) for p in range(acqs)]
    half = acqs * 4 * LINES

    def edge_copy(source, room, send, recv, target):
        return pltpu.make_async_remote_copy(
            source, room, edge_send.at[send], recv, device_id=target, device_id_type=MESH
        )

    to_inner = edge_copy(
        looks[0], edges.at[outer_room], 0, edge_recv.at[outer_room], {"strip": inner}
    )
    to_outer = edge_copy(
        looks[1], edges.at[inner_room], 1, edge_recv.at[inner_room], {"strip": outer}
    )
    to_relay = edge_copy(
        looks[0], relayed, 0, relay_recv.at[0], {"acq": acq - place, "strip": relay_out}
    )
    from_relay = edge_copy(
        relayed, edges.at[relay_room], 2, edge_recv.at[relay_room],
        {"acq": acq + from_place, "strip": relay_to},
    )

    def tap_columns(first):
        offset = first + iota((lines, LINES), 1) - iota((lines, LINES), 0)
        value = offset.astype(F32)
        inside = (offset >= -LINES) & (offset <= LINES)
        return jnp.where(inside, jnp.exp(-(value * value) / 32.0), 0.0)

    def azimuth(p, k, blocks, left):
        value = jnp.concatenate(
            [jnp.concatenate([block[p, k], block[p, k + 1]], axis=1) for block in blocks]
        )
        high = value.astype(BF16).astype(F32)
        right = jnp.concatenate([high, value - high, high])
        return jnp.dot(left, right.astype(BF16), preferred_element_type=F32)

    def azimuth_left(firsts):
        taps = jnp.concatenate([tap_columns(first) for first in firsts], axis=1)
        high = taps.astype(BF16).astype(F32)
        return jnp.concatenate([high, high, taps - high], axis=1).astype(BF16)

    late = {}
    early_left = azimuth_left([-LINES, lines, *first_line[:-1]])
    late_left = azimuth_left(first_line[-1:])

    for i, (g, start, count, first_part, last_part) in enumerate(chunks):
        if i == PASS_AT:

            @pl.when(passes_detour)
            def _():
                sent[detour].wait_recv()
                detour_on.start()

        if i == RELAY_AT:

            @pl.when(relays)
            def _():
                to_relay.wait_recv()
                from_relay.start()

        if i + DEPTH < len(chunks):
            own[i + DEPTH].wait()

        if i == DETOUR_AT:

            @pl.when(starts_detour)
            def _():
                pl.semaphore_wait(detour_ready, 1)
                sent[detour].start()

        if i + DEPTH < len(chunks):
            @pl.when(has_next)
            def _():
                sent[i].wait_send()

            @pl.when(has_next & jnp.logical_not(starts_detour) if i + DEPTH == detour else has_next)
            def _():
                sent[i + DEPTH].start()

        if i == len(chunks) - 2:
            edge_copy(
                looks[0], edges.at[inner_room], 0, edge_recv.at[inner_room], {"strip": inner}
            ).wait_recv()

            @pl.when(has_outer)
            def _():
                to_inner.wait_recv()

            blocks = [edges.at[0], edges.at[1], *looks[:-1]]
            for p in range(acqs):
                for k in range(0, 4, 2):
                    partial[p, k // 2] = azimuth(p, k, blocks, early_left)

        @pl.when(has_previous)
        def _():
            sent[i].wait_recv()

        piece = pieces[i]
        for t in range(count // TILE):
            here = pl.ds(t * TILE, TILE)
            there = pl.ds(start + t * TILE, TILE)
            for p in range(acqs):
                a, b = piece[slots[p], 0, :, here], piece[slots[p], 1, :, here]
                c, d = piece[reach + p, 0, :, here], piece[reach + p, 1, :, here]
                cosine, sine = table[p, 0, :, there], table[p, 1, :, there]
                x, y = a * c + b * d, b * c - a * d
                value = jnp.concatenate(
                    [x * cosine + y * sine, y * cosine - x * sine, a * a + b * b, c * c + d * d]
                )
                high, low = split(value)
                fields[pl.ds(p * 4 * LINES, 4 * LINES), here] = high
                fields[pl.ds(half + p * 4 * LINES, 4 * LINES), here] = low
        product = jnp.dot(
            fields[:, 0:count], weights[pl.ds(start, count), :], preferred_element_type=F32
        )
        part = (
            product[:half, :outputs] + product[:half, outputs:] + product[half:, :outputs]
        )
        if first_part:
            sums[...] = part
        elif not last_part:
            sums[...] += part
        if last_part:
            whole = part if first_part else sums[...] + part
            whole = whole.reshape(acqs, 4, LINES, outputs)
            room = late if g == groups - 1 else looks[g]
            for p in range(acqs):
                now = pl.ds(first_line[g], LINES)
                cosine, sine = line_table[p, 0, now, :], line_table[p, 1, now, :]
                x, y = whole[p, 0], whole[p, 1]
                room[p, 0] = x * cosine + y * sine
                room[p, 1] = y * cosine - x * sine
                room[p, 2] = whole[p, 2]
                room[p, 3] = whole[p, 3]
            if g == 0:

                @pl.when(crosses)
                def _():
                    pl.semaphore_wait(relay_ready, 1)
                    to_relay.start()

                @pl.when(jnp.logical_not(crosses))
                def _():
                    to_inner.start()

            if g == 1:

                @pl.when(has_outer)
                def _():
                    to_outer.start()

    for p in range(acqs):
        summed = []
        for k in range(0, 4, 2):
            value = partial[p, k // 2] + azimuth(p, k, [late], late_left)
            summed += [value[:, :outputs], value[:, outputs:]]
        scaling = lax.rsqrt(summed[2] * summed[3] + 1e-06)
        out[p, 0] = summed[0] * scaling
        out[p, 1] = summed[1] * scaling

    @pl.when(has_next)
    def _():
        for copy in sent[-DEPTH:]:
            copy.wait_send()

    @pl.when(passes_detour)
    def _():
        detour_on.wait_send()

    to_inner.wait_send()

    @pl.when(has_outer)
    def _():
        to_outer.wait_send()

    @pl.when(relays)
    def _():
        from_relay.wait_send()


def body(echoes, pair_list, phase_ramps):
    acqs, _, lines, width = echoes.shape
    groups = lines // LINES
    outputs = width // STEP
    chunks = chunk_list(groups)
    sizes = (acqs, groups, width, lax.axis_size("acq"), lax.axis_size("strip"))
    dma = pltpu.SemaphoreType.DMA
    look = pltpu.VMEM((acqs, 4, LINES, outputs), F32)
    return pl.pallas_call(
        functools.partial(kernel, sizes),
        out_shape=jax.ShapeDtypeStruct((acqs, 2, lines, outputs), F32),
        in_specs=[pl.BlockSpec(memory_space=pl.ANY)] * 3,
        out_specs=pl.BlockSpec(memory_space=pltpu.VMEM),
        scratch_shapes=[
            [pltpu.VMEM((2 * acqs - 1, 2, LINES, c[2]), F32) for c in chunks],
            pltpu.SMEM((2, acqs), I32),
            pltpu.SMEM((2, acqs), I32),
            pltpu.VMEM((width, 2 * outputs), BF16),
            pltpu.VMEM((acqs, 2, LINES, width), F32),
            pltpu.VMEM((acqs, 2, lines, outputs), F32),
            pltpu.VMEM((2 * acqs * 4 * LINES, max(c[2] for c in chunks)), BF16),
            pltpu.VMEM((acqs * 4 * LINES, outputs), F32),
            pltpu.VMEM((acqs, 2, lines, 2 * outputs), F32),
            [look for _ in range(groups)],
            pltpu.VMEM((2, acqs, 4, LINES, outputs), F32),
            look,
            dma((DEPTH,)),
            dma((len(chunks),)),
            dma((DEPTH,)),
            dma((3,)),
            dma((2,)),
            dma((1,)),
            dma((1,)),
            pltpu.SemaphoreType.REGULAR,
            pltpu.SemaphoreType.REGULAR,
        ],
        compiler_params=pltpu.CompilerParams(collective_id=0, has_side_effects=True, vmem_limit_bytes=16 << 20),
    )(*(pltpu.with_memory_space_constraint(v, pltpu.HBM) for v in (echoes, pair_list.T, phase_ramps.T)))


def solution(mesh):
    return jax.shard_map(
        body,
        mesh=mesh,
        in_specs=(P("acq", None, "strip", None), P("acq", None), P("acq", None)),
        out_specs=P("acq", None, "strip", None),
        check_vma=False,
    )
```
